32 devices in a mesh: strip: 8 (over z, x), col: 4 (over y, core).
Axes of the slice: x: 2, y: 2, z: 4, core: 2. Of those that a mesh axis runs over, the one named last changes fastest.
Arguments:
- net_box: int32 [32768, 4], P(('strip', 'col')), may hold values from 0 to 1023, as said below
- net_weight: float32 [32768], P(('strip', 'col')), may hold values from 0.5 to 2
- pin_bin: int32 [32768, 4, 2], P(('strip', 'col')), may hold values from 0 to 1023, as said below
- conv_first: bfloat16 [3, 3, 32, 3], replicated, may hold values from -1.25 to 1.25
- bias_first: float32 [32], replicated, may hold values from -3 to 3
- conv_second: bfloat16 [3, 3, 32, 32], replicated, may hold values from -0.375 to 0.375
- bias_second: float32 [32], replicated, may hold values from -3 to 3
- cotangent: bfloat16 [512, 32, 1024], P('col', None, 'strip'), may hold values from -6 to 6
Outputs:
- congestion: bfloat16 [512, 32, 1024], P('col', None, 'strip')
- net_grad: float32 [32768], P(('strip', 'col'))
The draws below stay inside these ranges and needn't reach their ends.
Inputs may be any that keep to these rules, and one draw needn't show every extreme that they name: `net_box`: box n = (x0, x1, y0, y1) has x0 <= x1 < x0 + 16 and y0 <= y1 < y0 + 16; y0 lies in rows s * 128 to (s + 1) * 128 - 1, where s = n // 4096 is the strip whose devices hold net n. Some box is 16 bins tall and wide. `pin_bin`: every pin of net n lies in net n's box.
All inputs are finite; a program needn't handle non-finite values.
Results may differ from the reference program's by a relative error of at most 0.0054.
Values may be sent and summed in bfloat16 or wider, within the bound.
No kernel may reach another device: no remote copies, remote signals or barrier semaphores. Data moves between devices by JAX's collectives and lax.ppermute only.
A program may use at most 192 MiB of HBM per device.

```python
import math
import jax
import jax.numpy as jnp
from jax import lax

RS = 128
NETS_DEV = 1024
PINS_NET = 4
BOX = 16
CH = 32
CIN = 3
NR = 1024
NC = 512
NETS = 32768
N_COL = 4


def geometry(key):
    subkeys = jax.random.split(jax.random.fold_in(key, 7), 6)
    net_index = jnp.arange(NETS, dtype=jnp.int32)
    strip_number = net_index // (NETS_DEV * N_COL)
    local_index = net_index % NETS_DEV
    offset = jax.random.randint(subkeys[0], (NETS,), 0, RS)
    offset = jnp.where(local_index == 0, 0, jnp.where(local_index == 1, RS - 1, offset))
    box_height = jax.random.randint(subkeys[1], (NETS,), 1, BOX + 1)
    box_width = jax.random.randint(subkeys[2], (NETS,), 1, BOX + 1)
    box_height = jnp.where(local_index == 0, BOX, box_height)
    box_width = jnp.where(local_index == 0, BOX, box_width)
    left_col = jax.random.randint(subkeys[3], (NETS,), 0, NC)
    left_col = jnp.where(local_index == 0, 0, jnp.where(local_index == 1, NC - 1, left_col))
    top_row = strip_number * RS + offset
    bottom_row = jnp.minimum(top_row + box_height - 1, NR - 1)
    right_col = jnp.minimum(left_col + box_width - 1, NC - 1)
    boxes_all = jnp.stack([left_col, right_col, top_row, bottom_row], axis=1).astype(jnp.int32)
    pin_rows = top_row[:, None] + jax.random.randint(subkeys[4], (NETS, PINS_NET), 0, (bottom_row - top_row + 1)[:, None])
    pin_cols = left_col[:, None] + jax.random.randint(subkeys[5], (NETS, PINS_NET), 0, (right_col - left_col + 1)[:, None])
    corner = (local_index == 0)[:, None] & (jnp.arange(PINS_NET, dtype=jnp.int32) == 0)[None, :]
    pin_rows = jnp.where(corner, top_row[:, None], pin_rows)
    pin_cols = jnp.where(corner, left_col[:, None], pin_cols)
    pins_all = jnp.stack([pin_rows, pin_cols], axis=2).astype(jnp.int32)
    return (boxes_all, pins_all)


def draw_net_box(key, part):
    return geometry(key)[0]


def draw_pin_bin(key, part):
    return geometry(key)[1]


def block_scale(rng, dims, shards, smallest, top_value):
    loudness = 1.0
    for dim, blocks in shards:
        draws = jax.random.uniform(jax.random.fold_in(jax.random.fold_in(rng, 6), dim), (blocks,), jnp.float32, smallest / len(shards), top_value / len(shards))
        loudness = loudness * jnp.repeat(jnp.exp(draws), dims[dim] // blocks).reshape((-1,) + (1,) * (len(dims) - 1 - dim))
    return loudness


def normal_values(key, extent, scale, reach, cuts=(), held_as=jnp.bfloat16):
    loudness = block_scale(key, extent, cuts, -0.22, 0.18) if cuts else 1.0
    entries = jax.random.normal(key, extent, jnp.float32) * scale * loudness
    return jnp.minimum(jnp.maximum(entries, -reach), reach).astype(held_as)


def setup_inputs(seed: int = 0) -> dict:
    arg_keys = jax.random.split(jax.random.key(seed), 9)
    net_box = draw_net_box(jax.random.fold_in(arg_keys[8], 71), 0)
    net_weight = jnp.clip(jnp.exp(math.log(2.0) - 1.3862944 * jax.random.uniform(arg_keys[1], (NETS,), jnp.float32) ** block_scale(arg_keys[1], (NETS,), ((0, 32),), -0.2, 0.2)), 0.5, 2.0)
    pin_bin = draw_pin_bin(jax.random.fold_in(arg_keys[8], 71), 0)
    conv_first = normal_values(arg_keys[3], (3, 3, CH, CIN), (9 * CIN) ** -0.5, 1.25)
    bias_first = normal_values(arg_keys[4], (CH,), 0.5, 3.0, (), jnp.float32)
    conv_second = normal_values(arg_keys[5], (3, 3, CH, CH), (9 * CH) ** -0.5, 0.375)
    bias_second = normal_values(arg_keys[6], (CH,), 0.5, 3.0, (), jnp.float32)
    cotangent = normal_values(arg_keys[7], (NC, CH, NR), 1.0, 6.0, ((0, 4), (2, 8)))
    return dict(net_box=net_box, net_weight=net_weight, pin_bin=pin_bin, conv_first=conv_first, bias_first=bias_first, conv_second=conv_second, bias_second=bias_second, cotangent=cotangent)


def silu_slope(pre_act):
    sigmoid = jax.nn.sigmoid(pre_act)
    return sigmoid * (1.0 + pre_act * (1.0 - sigmoid))


def conv_valid(padded, weights, out_cols, out_rows):
    summed = None
    for shift_row in range(3):
        for shift_col in range(3):
            window = padded[shift_col:shift_col + out_cols, :, shift_row:shift_row + out_rows].astype(jnp.float32)
            product = jnp.einsum("oi,xiy->xoy", weights[shift_row, shift_col].astype(jnp.float32), window)
            summed = product if summed is None else summed + product
    return summed


def conv_back(padded, weights, out_cols, out_rows):
    summed = None
    for shift_row in range(3):
        for shift_col in range(3):
            window = padded[2 - shift_col:2 - shift_col + out_cols, :, 2 - shift_row:2 - shift_row + out_rows].astype(jnp.float32)
            product = jnp.einsum("oi,xoy->xiy", weights[shift_row, shift_col].astype(jnp.float32), window)
            summed = product if summed is None else summed + product
    return summed


def reference(net_box, net_weight, pin_bin, conv_first, bias_first, conv_second, bias_second, cotangent):
    left_col = net_box[:, 0]
    right_col = net_box[:, 1]
    top_row = net_box[:, 2]
    bottom_row = net_box[:, 3]
    box_height = (bottom_row - top_row + 1).astype(jnp.float32)
    box_width = (right_col - left_col + 1).astype(jnp.float32)
    rounded = jnp.stack([net_weight / box_height, net_weight / box_width], axis=0).astype(jnp.bfloat16)
    values = lax.optimization_barrier(rounded).astype(jnp.float32)
    offsets = jnp.arange(BOX, dtype=jnp.int32)
    row_grid = top_row[:, None] + offsets[None, :]
    in_box = row_grid <= bottom_row[:, None]
    row_grid = jnp.minimum(row_grid, NR - 1)
    demand = values[:, :, None] * in_box[None].astype(jnp.float32)
    channel = jnp.arange(2, dtype=jnp.int32)[:, None, None]
    edges_map = jnp.zeros((2, NR, NC + 1), jnp.float32)
    edges_map = edges_map.at[channel, row_grid[None], left_col[None, :, None]].add(demand)
    edges_map = edges_map.at[channel, row_grid[None], right_col[None, :, None] + 1].add(-demand)
    rudy_maps = jnp.cumsum(edges_map, axis=2)[:, :, :NC]
    pin_map = jnp.zeros((NR, NC), jnp.float32).at[pin_bin[:, :, 0].reshape(-1), pin_bin[:, :, 1].reshape(-1)].add(1.0)
    features = jnp.stack([rudy_maps[0], rudy_maps[1], pin_map], axis=0)
    features = jnp.transpose(features, (2, 0, 1)).astype(jnp.bfloat16)
    feature_pad = jnp.pad(features, ((2, 2), (0, 0), (2, 2)))
    cot_pad = jnp.pad(cotangent, ((2, 2), (0, 0), (2, 2)))
    block_cols = math.gcd(NC, 256)

    def one_block(block_start):
        feature_block = lax.dynamic_slice_in_dim(feature_pad, block_start, block_cols + 4, 0)
        cot_block = lax.dynamic_slice_in_dim(cot_pad, block_start, block_cols + 4, 0)
        col_ids = block_start - 1 + jnp.arange(block_cols + 2, dtype=jnp.int32)
        row_ids = jnp.arange(NR + 2, dtype=jnp.int32) - 1
        inside = ((col_ids >= 0) & (col_ids < NC))[:, None, None] & ((row_ids >= 0) & (row_ids < NR))[None, None, :]
        pre_act = conv_valid(feature_block, conv_first, block_cols + 2, NR + 2) + bias_first[None, :, None]
        hidden = jnp.where(inside, jax.nn.silu(pre_act), 0.0).astype(jnp.bfloat16)
        congestion = (conv_valid(hidden, conv_second, block_cols, NR) + bias_second[None, :, None]).astype(jnp.bfloat16)
        back_hidden = conv_back(cot_block, conv_second, block_cols + 2, NR + 2)
        back_pre = jnp.where(inside, back_hidden * silu_slope(pre_act), 0.0).astype(jnp.bfloat16)
        back_maps = conv_back(back_pre, conv_first[:, :, :, :2], block_cols, NR).astype(jnp.bfloat16)
        return congestion, back_maps

    starts = jnp.arange(NC // block_cols, dtype=jnp.int32) * block_cols
    congestion, back_maps = lax.map(one_block, starts)
    congestion = congestion.reshape(NC, CH, NR)
    back_maps = back_maps.reshape(NC, 2, NR)
    grad_maps = jnp.transpose(back_maps.astype(jnp.float32), (1, 2, 0))
    prefix = jnp.concatenate([jnp.zeros((2, NR, 1), jnp.float32), jnp.cumsum(grad_maps, axis=2)], axis=2)
    row_sums = prefix[:, row_grid, right_col[:, None] + 1] - prefix[:, row_grid, left_col[:, None]]
    net_grad = jnp.sum(in_box.astype(jnp.float32) * (row_sums[0] / box_height[:, None] + row_sums[1] / box_width[:, None]), axis=1)
    return congestion, net_grad
```

```python
import functools

import jax
import jax.numpy as jnp
from jax import lax
from jax.experimental import pallas as pl
from jax.experimental.pallas import tpu as pltpu
from jax.sharding import PartitionSpec as P

F32 = jnp.float32
BF16 = jnp.bfloat16
BOX = 16
REACH = BOX + 1
LANES = 256
NROWS = 144
JCOLS = 144
FIELDS = 16
GROUP = 6
WINDOW = 8
EDGE = 24
VMEM = 56 * 1024 * 1024

NN = (((1,), (0,)), ((), ()))
NT = (((1,), (1,)), ((), ()))
TN = (((0,), (0,)), ((), ()))


def dot(a, b, dims=NN):
    return lax.dot_general(a, b, dims, preferred_element_type=F32)


def iota(shape, dim):
    return lax.broadcasted_iota(jnp.int32, shape, dim)


def onehot(pred):
    return jnp.where(pred, 1.0, 0.0).astype(BF16)


def call(body, out, n_in, scratch=(), cost=None, in_specs=None):
    whole = pl.BlockSpec(memory_space=pltpu.VMEM)
    outs = jax.tree.map(lambda x: whole, out)
    return pl.pallas_call(
        body,
        out_shape=out,
        in_specs=in_specs or [whole] * n_in,
        out_specs=outs,
        scratch_shapes=list(scratch),
        compiler_params=pltpu.CompilerParams(vmem_limit_bytes=VMEM),
        cost_estimate=cost,
    )


def cost(flops, nbytes):
    return pl.CostEstimate(flops=flops, bytes_accessed=nbytes, transcendentals=0)


def pack_body(pins, box, weight, pin, first, last, to_right, to_left, plain):
    rows = [box[...].astype(F32), weight[...]]
    rows += [pin[p].astype(F32) for p in range(pins)]
    nets = box.shape[1]
    used = 5 + 2 * pins
    rows.append(jnp.zeros((FIELDS - used, nets), F32))
    fields = jnp.concatenate(rows, axis=0)
    plain[...] = fields
    to_right[0:FIELDS, :] = fields
    to_left[0:FIELDS, :] = fields
    for ref, edge in ((to_right, last), (to_left, first)):
        e = edge[...].astype(F32)
        for k in range(8):
            ref[FIELDS : FIELDS + 8, 128 * k : 128 * (k + 1)] = e[8 * k : 8 * k + 8, :]


def cot_edge_body(cot, up, down):
    span = cot.shape[1]
    m = iota((32, span), 0)
    lane = iota((32, span), 1)
    sel = onehot(((m < REACH) & (lane == m)) | ((m >= EDGE) & (lane == span - 2 + m - EDGE)))
    step = 512
    for k in range(cot.shape[0] // step):
        got = dot(sel, cot[step * k : step * (k + 1), :], NT).astype(BF16)
        up[:, step * k : step * (k + 1)] = got[:EDGE]
        down[:, step * k : step * (k + 1)] = got[EDGE:]


def weight_body(second, first, fwd, bwd, first_fwd, first_bwd):
    chans = second.shape[1]
    tile = onehot(iota((chans, WINDOW * chans), 1) % chans == iota((chans, WINDOW * chans), 0))
    lane_t = iota((chans, WINDOW * chans), 1) // chans
    cin = first.shape[1]
    ftile = onehot(iota((cin, cin * 16), 1) // 16 == iota((cin, cin * 16), 0))
    ft = iota((chans, cin * 16), 1) % 16
    row8 = iota((8, WINDOW * chans), 0)
    lane8 = iota((8, WINDOW * chans), 1) // chans
    for r in range(3):
        taps = [dot(second[3 * r + c], tile) for c in range(3)]
        flipped = [dot(second[3 * r + c], tile, TN) for c in range(3)]
        for jo in range(GROUP):
            lo = (r * GROUP + jo) * chans
            acc = jnp.zeros((chans, WINDOW * chans), F32)
            acc2 = acc
            for c in range(3):
                acc = jnp.where(lane_t == jo + c, taps[c], acc)
                acc2 = jnp.where(lane_t == jo + 2 - c, flipped[c], acc2)
            fwd[lo : lo + chans, :] = acc.astype(BF16)
            bwd[lo : lo + chans, :] = acc2.astype(BF16)
        ftaps = [dot(first[3 * r + c], ftile, TN) for c in range(3)]
        parts = []
        for jo in range(8):
            acc = jnp.zeros((chans, cin * 16), F32)
            for c in range(3):
                acc = jnp.where(ft == jo + c, ftaps[c], acc)
            parts.append(acc)
        first_fwd[r] = jnp.concatenate(parts, axis=0).astype(BF16)
        fback = [dot(first[3 * r + c], tile) for c in range(3)]
        for ch in range(2):
            acc = jnp.zeros((8, WINDOW * chans), F32)
            for c in range(3):
                row = jnp.broadcast_to(fback[c][ch : ch + 1, :], acc.shape)
                acc = jnp.where((lane8 == row8 + 2 - c) & (row8 < GROUP), row, acc)
            first_bwd[16 * r + 8 * ch : 16 * r + 8 * ch + 8, :] = acc


def relative(ref, m, col0, row0):
    f = ref[m, 0:FIELDS, :]
    x = lambda v: jnp.clip(v - (col0 - 2.0), -2.0, 250.0)
    y = lambda v: jnp.clip(v - row0, -2.0, 250.0)
    return f, x, y


def raster_body(pins, n_nets, *refs):
    pos = refs[0]
    net_refs = refs[1 : 1 + n_nets]
    left_ref, right_ref, maps, up, down = refs[1 + n_nets :]
    col0 = pos[0].astype(F32)
    row0 = pos[1].astype(F32)
    maps[...] = jnp.zeros_like(maps)
    nets = net_refs[0].shape[2]
    step = nets
    jcol = iota((JCOLS, step), 0).astype(F32).astype(BF16)
    one = jnp.ones((), BF16)
    zero = jnp.zeros((), BF16)

    def chunk(ref, m):
        f, x, y = relative(ref, m, col0, row0)
        x0, x1 = x(f[0:1]).astype(BF16), x(f[1:2]).astype(BF16)
        y0, y1 = y(f[2:3]).astype(BF16), y(f[3:4]).astype(BF16)
        vh = (f[4:5] / (f[3:4] - f[2:3] + 1.0)).astype(BF16)
        vv = (f[4:5] / (f[1:2] - f[0:1] + 1.0)).astype(BF16)
        in_col = (x0 <= jcol) & (jcol <= x1)
        in_row = jnp.where((y0 <= jcol) & (jcol <= y1), one, zero)
        maps[0, :, 0:NROWS] += dot(jnp.where(in_col, vh, zero), in_row, NT)
        maps[1, :, 0:NROWS] += dot(jnp.where(in_col, vv, zero), in_row, NT)
        acc = jnp.zeros((JCOLS, NROWS), F32)
        for p in range(pins):
            py = y(f[5 + 2 * p : 6 + 2 * p]).astype(BF16)
            px = x(f[6 + 2 * p : 7 + 2 * p]).astype(BF16)
            acc += dot(
                jnp.where(px == jcol, one, zero), jnp.where(py == jcol, one, zero), NT
            )
        maps[2, :, 0:NROWS] += acc

    for ref in net_refs:
        if ref.shape[0] == 1:
            chunk(ref, 0)
        else:
            lax.fori_loop(0, ref.shape[0], lambda m, c: (chunk(ref, m), c)[1], 0)
    span = left_ref.shape[1]
    m = iota((EDGE, LANES), 0)
    lane = iota((EDGE, LANES), 1)
    sel_up = onehot((m < REACH) & (lane == m))
    sel_dn = onehot((m < REACH) & (lane == span - 2 + m))
    side = jnp.concatenate([left_ref[...], right_ref[...]], axis=0)
    side = jnp.concatenate([side, jnp.zeros((side.shape[0], LANES - span), BF16)], axis=1)
    feat = maps[...].reshape(3 * JCOLS, LANES).astype(BF16)
    n = 3 * JCOLS
    for sel, out in ((sel_up, up), (sel_dn, down)):
        out[:, 0:n] = dot(sel, feat, NT).astype(BF16)
        out[:, n:] = dot(sel, side, NT).astype(BF16)


def network_body(
    pins, n_nets, *refs
):
    pos = refs[0]
    net_refs = refs[1 : 1 + n_nets]
    (
        maps, from_up, from_down, cot, cot_below, cot_above, left_ref, right_ref,
        fwd, bwd, first_fwd, first_bwd, bias1, bias2,
    ) = refs[1 + n_nets : 15 + n_nets]
    rest = refs[15 + n_nets :]
    congestion = rest[0]
    grads = rest[1 : 1 + n_nets]
    cotx, feats, back_h, hid, back_p, grad_maps = rest[1 + n_nets :]
    chans = bias1.shape[0]
    span = cot.shape[1]
    cols = cot.shape[0] // chans
    col0, row0, all_cols, all_rows = pos[0], pos[1], pos[2], pos[3]
    n = 3 * JCOLS

    e = jnp.concatenate([from_up[...], from_down[...]], axis=0)
    m = iota((2 * EDGE, LANES), 0)
    lane = iota((2 * EDGE, LANES), 1)
    place = onehot(
        ((m < REACH) & (lane == (m - 2) % LANES))
        | ((m >= EDGE) & (m < EDGE + REACH) & (lane == span + m - EDGE))
    )
    total = maps[...].reshape(n, LANES) + dot(e[:, 0:n], place, TN)
    total = total.astype(BF16).astype(F32).reshape(3, JCOLS, LANES)
    feats[1] = total
    feats[0] = pltpu.roll(total, 1, 2)
    feats[2] = pltpu.roll(total, LANES - 1, 2)

    mm = iota((32, span), 0)
    ll = iota((32, span), 1)
    place2 = onehot(((mm < REACH) & (ll == mm)) | ((mm >= EDGE) & (ll == span - 2 + mm - EDGE)))
    first_row = 2 * chans
    cotx[first_row : first_row + cols * chans, 0:span] = cot[...]
    step = 512
    for k in range(cols * chans // step):
        s = slice(step * k, step * (k + 1))
        ends = jnp.concatenate([cot_below[:, s], cot_above[:, s]], axis=0)
        cotx[first_row + step * k : first_row + step * (k + 1), span:LANES] = dot(
            ends, place2, TN
        ).astype(BF16)
    edge_place = dot(e[:, n:], jnp.where(m < EDGE, jnp.where(m < 2, place, 0), place), TN).astype(BF16)
    tail = first_row + cols * chans
    cotx[0:first_row, 0:span] = left_ref[...]
    cotx[0:first_row, span:LANES] = edge_place[0:first_row, span:LANES]
    cotx[tail : tail + first_row, 0:span] = right_ref[...]
    cotx[tail : tail + first_row, span:LANES] = edge_place[first_row : 2 * first_row, span:LANES]
    cotx[tail + first_row :, :] = jnp.zeros((cotx.shape[0] - tail - first_row, LANES), BF16)

    block = GROUP * chans
    window = WINDOW * chans
    groups = pl.cdiv(cols + 2, GROUP)
    back_h[groups * block :, :] = jnp.zeros((back_h.shape[0] - groups * block, LANES), F32)

    def step_a(g, carry):
        lo = pl.multiple_of(g * block, block)
        p = dot(bwd[...], cotx[pl.ds(lo, window), :])
        back_h[pl.ds(lo, block), :] = (
            p[block : 2 * block]
            + pltpu.roll(p[0:block], LANES - 1, 1)
            + pltpu.roll(p[2 * block :], 1, 1)
        )
        return carry

    lax.fori_loop(0, groups, step_a, 0)

    lanes1 = iota((1, LANES), 1)
    row_of = jnp.where(lanes1 < LANES - 64, lanes1, lanes1 - LANES)
    grow = row_of + row0
    row_ok = (row_of >= -1) & (row_of < span + BOX) & (grow >= 0) & (grow < all_rows)
    bias_col = bias1[...].astype(F32)
    bias_rep = jnp.concatenate([bias_col] * 8, axis=0)
    jo_rows = iota((8 * chans, 1), 0) // chans

    def step_b(g, carry):
        lo8 = pl.multiple_of(g * 8, 8)
        pre = bias_rep
        for r in range(3):
            f = feats[r, :, pl.ds(lo8, 16), :].reshape(3 * 16, LANES).astype(BF16)
            pre = pre + dot(first_fwd[r], f)
        lo = pl.multiple_of(g * 8 * chans, 8 * chans)
        slot = 8 * g + 1 + jo_rows
        gcol = slot - 2 + col0
        col_ok = (slot <= cols + 2) & (gcol >= 0) & (gcol < all_cols)
        ok = col_ok & row_ok
        s = 0.5 + 0.5 * jnp.tanh(0.5 * pre)
        h = pre * s
        slope = s + h * (1.0 - s)
        bh = back_h[pl.ds(lo, 8 * chans), :]
        hid[pl.ds(lo, 8 * chans), :] = jnp.where(ok, h, 0.0).astype(BF16)
        back_p[pl.ds(lo, 8 * chans), :] = jnp.where(ok, bh * slope, 0.0).astype(BF16)
        return carry

    lax.fori_loop(0, pl.cdiv(cols + 2, 8), step_b, 0)

    bias_out = jnp.concatenate([bias2[...]] * GROUP, axis=0)
    groups_c = pl.cdiv(cols, GROUP)

    def back(g, lo):
        q = dot(first_bwd[...].astype(BF16), back_p[pl.ds(lo, window), :])
        gm = q[16:32] + pltpu.roll(q[0:16], LANES - 1, 1) + pltpu.roll(q[32:48], 1, 1)
        grad_maps[pl.ds(pl.multiple_of(16 * g, 16), 16), :] = gm.astype(BF16)

    def conv(lo):
        p = dot(fwd[...], hid[pl.ds(lo, window), :])
        out = (
            p[block : 2 * block]
            + pltpu.roll(p[0:block], 1, 1)
            + pltpu.roll(p[2 * block :], LANES - 1, 1)
        )
        return (out[:, 0:span] + bias_out).astype(BF16)

    def step_c(g, carry):
        lo = pl.multiple_of(g * block, block)
        congestion[pl.ds(lo, block), :] = conv(lo)
        back(g, lo)
        return carry

    full = cols // GROUP
    lax.fori_loop(0, full, step_c, 0)
    if groups_c > full:
        lo = full * block
        last = (cols - full * GROUP) * chans
        congestion[lo : lo + last, :] = conv(lo)[0:last]
        back(full, lo)

    x_rows = iota((8 * groups_c, 1), 0)
    slot = GROUP * (x_rows // 8) + x_rows % 8 + 2
    slot = jnp.where((x_rows % 8 < GROUP) & (slot < cols + 2), slot, 512).astype(F32)
    nets = net_refs[0].shape[2]
    fcol = col0.astype(F32)
    frow = row0.astype(F32)
    rows = iota((NROWS, nets), 0).astype(F32).astype(BF16)
    one = jnp.ones((), BF16)
    zero = jnp.zeros((), BF16)

    def net_chunk(ref, out, k):
        f, x, y = relative(ref, k, fcol, frow)
        y0, y1 = y(f[2:3]).astype(BF16), y(f[3:4]).astype(BF16)
        in_row = jnp.where((y0 <= rows) & (rows <= y1), one, zero)
        h = dot(grad_maps[:, 0:NROWS], in_row).reshape(groups_c, 2, 8, nets)
        x0, x1 = x(f[0:1]), x(f[1:2])
        in_col = ((x0 <= slot) & (slot <= x1)).reshape(groups_c, 8, nets)
        s0 = jnp.sum(jnp.sum(jnp.where(in_col, h[:, 0], 0.0), axis=0), axis=0, keepdims=True)
        s1 = jnp.sum(jnp.sum(jnp.where(in_col, h[:, 1], 0.0), axis=0), axis=0, keepdims=True)
        out[k, 0:1, :] = s0 / (f[3:4] - f[2:3] + 1.0) + s1 / (f[1:2] - f[0:1] + 1.0)

    for ref, out in zip(net_refs, grads):
        if ref.shape[0] == 1:
            net_chunk(ref, out, 0)
        else:
            lax.fori_loop(0, ref.shape[0], lambda k, c: (net_chunk(ref, out, k), c)[1], 0)


def shards(
    net_box, net_weight, pin_bin, conv_first, bias_first, conv_second, bias_second, cotangent
):
    cols, chans, span = cotangent.shape
    nets, pins = pin_bin.shape[:2]
    strips = lax.axis_size("strip")
    ncol = lax.axis_size("col")
    strip_index = lax.axis_index("strip")
    col_index = lax.axis_index("col")
    pos = jnp.stack(
        [col_index * cols, strip_index * span, cols * ncol, span * strips]
    ).astype(jnp.int32)
    cot = cotangent.reshape(cols * chans, span)
    edge = 2 * chans
    one_block = pl.BlockSpec((edge, span), lambda i: (0, 0))
    last_block = pl.BlockSpec((edge, span), lambda i: (cols * chans // edge - 1, 0))

    def full(*shape):
        return pl.BlockSpec(shape, lambda i: (0,) * len(shape))

    right, left, plain = pl.pallas_call(
        functools.partial(pack_body, pins),
        grid=(1,),
        in_specs=[full(4, nets), full(1, nets), full(pins, 2, nets), one_block, last_block],
        out_specs=[full(FIELDS + 8, nets), full(FIELDS + 8, nets), full(FIELDS, nets)],
        out_shape=[
            jax.ShapeDtypeStruct((FIELDS + 8, nets), F32),
            jax.ShapeDtypeStruct((FIELDS + 8, nets), F32),
            jax.ShapeDtypeStruct((FIELDS, nets), F32),
        ],
        cost_estimate=cost(10000, 400000),
    )(net_box.T, net_weight.reshape(1, nets), pin_bin.transpose(1, 2, 0), cot, cot)

    def ring(k):
        return [(i, (i + k) % ncol) for i in range(ncol)]

    from_left = lax.ppermute(right, "col", ring(1))
    from_right = lax.ppermute(left, "col", ring(ncol - 1))
    few = ncol == 4
    if few:
        far = lax.ppermute(plain, "col", ring(2))
        groups = [plain[None], from_left[None], from_right[None], far[None]]
    else:
        groups = [lax.all_gather(plain, "col", axis=0)]

    def unpack(buf, has):
        e = buf[FIELDS:].reshape(8, 8, span).transpose(1, 0, 2).reshape(edge, span)
        return jnp.where(has, e, 0.0).astype(BF16)

    left_cols = unpack(from_left, col_index > 0)
    right_cols = unpack(from_right, col_index < ncol - 1)
    up_pairs = [(i + 1, i) for i in range(strips - 1)]
    down_pairs = [(i, i + 1) for i in range(strips - 1)]

    cot_up, cot_down = call(
        cot_edge_body,
        [
            jax.ShapeDtypeStruct((EDGE, cols * chans), BF16),
            jax.ShapeDtypeStruct((8, cols * chans), BF16),
        ],
        1,
        cost=cost(40000000, 1300000),
    )(cot)
    cot_below = lax.ppermute(cot_up, "strip", up_pairs)
    cot_above = lax.ppermute(cot_down, "strip", down_pairs)

    cin = conv_first.shape[3]
    weights = call(
        weight_body,
        [
            jax.ShapeDtypeStruct((3 * GROUP * chans, WINDOW * chans), BF16),
            jax.ShapeDtypeStruct((3 * GROUP * chans, WINDOW * chans), BF16),
            jax.ShapeDtypeStruct((3, 8 * chans, cin * 16), BF16),
            jax.ShapeDtypeStruct((48, WINDOW * chans), F32),
        ],
        2,
        cost=cost(40000000, 1000000),
    )(
        conv_second.reshape(9, chans, chans),
        conv_first.reshape(9, chans, cin).transpose(0, 2, 1),
    )

    smem = pl.BlockSpec(memory_space=pltpu.SMEM)
    vmem = pl.BlockSpec(memory_space=pltpu.VMEM)
    width = 3 * JCOLS + 2 * edge
    maps, up, down = call(
        functools.partial(raster_body, pins, len(groups)),
        [
            jax.ShapeDtypeStruct((3, JCOLS, LANES), F32),
            jax.ShapeDtypeStruct((EDGE, width), BF16),
            jax.ShapeDtypeStruct((EDGE, width), BF16),
        ],
        0,
        in_specs=[smem] + [vmem] * (len(groups) + 2),
        cost=cost(1500000000, 1500000),
    )(pos, *groups, left_cols, right_cols)

    from_down = lax.ppermute(up, "strip", up_pairs)
    from_up = lax.ppermute(down, "strip", down_pairs)

    rows_x = (cols + 16) * chans
    outs = call(
        functools.partial(network_body, pins, len(groups)),
        [jax.ShapeDtypeStruct((cols * chans, span), BF16)]
        + [jax.ShapeDtypeStruct((g.shape[0], 1, nets), F32) for g in groups],
        0,
        in_specs=[smem] + [vmem] * (len(groups) + 14),
        scratch=[
            pltpu.VMEM((rows_x, LANES), BF16),
            pltpu.VMEM((3, 3, JCOLS, LANES), F32),
            pltpu.VMEM((rows_x, LANES), F32),
            pltpu.VMEM((rows_x, LANES), BF16),
            pltpu.VMEM((rows_x, LANES), BF16),
            pltpu.VMEM((16 * pl.cdiv(cols, GROUP), LANES), BF16),
        ],
        cost=cost(3000000000, 4000000),
    )(
        pos, *groups, maps, from_up, from_down, cot, cot_below, cot_above,
        left_cols, right_cols, *weights,
        bias_first.reshape(chans, 1), bias_second.reshape(chans, 1),
    )
    congestion = outs[0].reshape(cols, chans, span)
    if few:
        own, to_left, to_right, to_far = outs[1:]
        net_grad = (
            own
            + lax.ppermute(to_left, "col", ring(3))
            + lax.ppermute(to_right, "col", ring(1))
            + lax.ppermute(to_far, "col", ring(2))
        )
    else:
        net_grad = lax.psum_scatter(outs[1], "col", scatter_dimension=0, tiled=True)
    return congestion, net_grad.reshape(nets)


def solution(mesh):
    placed = (
        P(("strip", "col"), None),
        P(("strip", "col")),
        P(("strip", "col"), None, None),
        P(),
        P(),
        P(),
        P(),
        P("col", None, "strip"),
    )
    return jax.shard_map(
        shards,
        mesh=mesh,
        in_specs=placed,
        out_specs=(P("col", None, "strip"), P(("strip", "col"))),
        check_vma=False,
    )
```

```python
import functools

import jax
import jax.numpy as jnp
from jax import lax
from jax.experimental import pallas as pl
from jax.experimental.pallas import tpu as pltpu
from jax.sharding import PartitionSpec as P

F32 = jnp.float32
BF16 = jnp.bfloat16
BOX = 16
REACH = BOX + 1
LANES = 256
NROWS = 144
JCOLS = 144
FIELDS = 16
GROUP = 6
WINDOW = 8
EDGE = 24
VMEM = 56 * 1024 * 1024

NN = (((1,), (0,)), ((), ()))
NT = (((1,), (1,)), ((), ()))
TN = (((0,), (0,)), ((), ()))


def dot(a, b, dims=NN):
    return lax.dot_general(a, b, dims, preferred_element_type=F32)


def iota(shape, dim):
    return lax.broadcasted_iota(jnp.int32, shape, dim)


def onehot(pred):
    return jnp.where(pred, 1.0, 0.0).astype(BF16)


def call(body, out, n_in, scratch=(), cost=None, in_specs=None):
    whole = pl.BlockSpec(memory_space=pltpu.VMEM)
    outs = jax.tree.map(lambda x: whole, out)
    return pl.pallas_call(
        body,
        out_shape=out,
        in_specs=in_specs or [whole] * n_in,
        out_specs=outs,
        scratch_shapes=list(scratch),
        compiler_params=pltpu.CompilerParams(vmem_limit_bytes=VMEM),
        cost_estimate=cost,
    )


def cost(flops, nbytes):
    return pl.CostEstimate(flops=flops, bytes_accessed=nbytes, transcendentals=0)


def pack_body(pins, box, weight, pin, first, last, to_even, to_odd, plain):
    odd = lax.axis_index("col") % 2 == 1
    rows = [box[...].astype(F32), weight[...]]
    rows += [pin[p].astype(F32) for p in range(pins)]
    nets = box.shape[1]
    used = 5 + 2 * pins
    rows.append(jnp.zeros((FIELDS - used, nets), F32))
    fields = jnp.concatenate(rows, axis=0)
    plain[...] = fields
    to_even[0:FIELDS, :] = fields
    to_odd[0:FIELDS, :] = fields
    a, b = first[...].astype(F32), last[...].astype(F32)
    for ref, e in ((to_even, jnp.where(odd, a, b)), (to_odd, jnp.where(odd, b, a))):
        for k in range(8):
            ref[FIELDS : FIELDS + 8, 128 * k : 128 * (k + 1)] = e[8 * k : 8 * k + 8, :]


def cot_edge_body(cot, to_even, to_odd):
    odd = lax.axis_index("strip") % 2
    span = cot.shape[1]
    m = iota((2 * EDGE, span), 0)
    lane = iota((2 * EDGE, span), 1)
    up = (m % EDGE < REACH) & (lane == m % EDGE)
    down = (m % EDGE < 2) & (lane == span - 2 + m % EDGE)
    sel = onehot(((m // EDGE == odd) & down) | ((m // EDGE != odd) & up))
    step = 512
    for k in range(cot.shape[0] // step):
        got = dot(sel, cot[step * k : step * (k + 1), :], NT).astype(BF16)
        to_even[:, step * k : step * (k + 1)] = got[:EDGE]
        to_odd[:, step * k : step * (k + 1)] = got[EDGE:]


def block_origin(cols, span):
    return lax.axis_index("col") * cols, lax.axis_index("strip") * span


def side_columns(even_ref, odd_ref, span):
    c = lax.axis_index("col")
    odd = c % 2 == 1

    def unpack(ref):
        e = ref[0, FIELDS : FIELDS + 8, :]
        return jnp.concatenate([e[:, span * k : span * (k + 1)] for k in range(8)], axis=0)

    a, b = unpack(even_ref), unpack(odd_ref)
    left = jnp.where(c > 0, jnp.where(odd, a, b), 0.0)
    right = jnp.where(c < lax.axis_size("col") - 1, jnp.where(odd, b, a), 0.0)
    return left.astype(BF16), right.astype(BF16)


def weight_body(second, first, fwd, bwd, first_fwd, first_bwd):
    chans = second.shape[1]
    tile = onehot(iota((chans, WINDOW * chans), 1) % chans == iota((chans, WINDOW * chans), 0))
    lane_t = iota((chans, WINDOW * chans), 1) // chans
    cin = first.shape[1]
    ftile = onehot(iota((cin, cin * 16), 1) // 16 == iota((cin, cin * 16), 0))
    ft = iota((chans, cin * 16), 1) % 16
    row8 = iota((8, WINDOW * chans), 0)
    lane8 = iota((8, WINDOW * chans), 1) // chans
    for r in range(3):
        taps = [dot(second[3 * r + c], tile) for c in range(3)]
        flipped = [dot(second[3 * r + c], tile, TN) for c in range(3)]
        for jo in range(GROUP):
            lo = (r * GROUP + jo) * chans
            acc = jnp.zeros((chans, WINDOW * chans), F32)
            acc2 = acc
            for c in range(3):
                acc = jnp.where(lane_t == jo + c, taps[c], acc)
                acc2 = jnp.where(lane_t == jo + 2 - c, flipped[c], acc2)
            fwd[lo : lo + chans, :] = acc.astype(BF16)
            bwd[lo : lo + chans, :] = acc2.astype(BF16)
        ftaps = [dot(first[3 * r + c], ftile, TN) for c in range(3)]
        parts = []
        for jo in range(8):
            acc = jnp.zeros((chans, cin * 16), F32)
            for c in range(3):
                acc = jnp.where(ft == jo + c, ftaps[c], acc)
            parts.append(acc)
        first_fwd[r] = jnp.concatenate(parts, axis=0).astype(BF16)
        fback = [dot(first[3 * r + c], tile) for c in range(3)]
        for ch in range(2):
            acc = jnp.zeros((8, WINDOW * chans), F32)
            for c in range(3):
                row = jnp.broadcast_to(fback[c][ch : ch + 1, :], acc.shape)
                acc = jnp.where((lane8 == row8 + 2 - c) & (row8 < GROUP), row, acc)
            first_bwd[16 * r + 8 * ch : 16 * r + 8 * ch + 8, :] = acc


def relative(ref, m, col0, row0):
    f = ref[m, 0:FIELDS, :]
    x = lambda v: jnp.clip(v - (col0 - 2.0), -2.0, 250.0)
    y = lambda v: jnp.clip(v - row0, -2.0, 250.0)
    return f, x, y


def raster_body(pins, cols, span, n_nets, *refs):
    net_refs = refs[:n_nets]
    even_ref, odd_ref, maps, to_even, to_odd = refs[n_nets:]
    col0, row0 = (v.astype(F32) for v in block_origin(cols, span))
    maps[...] = jnp.zeros_like(maps)
    nets = net_refs[0].shape[2]
    step = nets
    jcol = iota((JCOLS, step), 0).astype(F32).astype(BF16)
    one = jnp.ones((), BF16)
    zero = jnp.zeros((), BF16)

    def chunk(ref, m):
        f, x, y = relative(ref, m, col0, row0)
        x0, x1 = x(f[0:1]).astype(BF16), x(f[1:2]).astype(BF16)
        y0, y1 = y(f[2:3]).astype(BF16), y(f[3:4]).astype(BF16)
        vh = (f[4:5] / (f[3:4] - f[2:3] + 1.0)).astype(BF16)
        vv = (f[4:5] / (f[1:2] - f[0:1] + 1.0)).astype(BF16)
        in_col = (x0 <= jcol) & (jcol <= x1)
        in_row = jnp.where((y0 <= jcol) & (jcol <= y1), one, zero)
        maps[0, :, 0:NROWS] += dot(jnp.where(in_col, vh, zero), in_row, NT)
        maps[1, :, 0:NROWS] += dot(jnp.where(in_col, vv, zero), in_row, NT)
        acc = jnp.zeros((JCOLS, NROWS), F32)
        for p in range(pins):
            py = y(f[5 + 2 * p : 6 + 2 * p]).astype(BF16)
            px = x(f[6 + 2 * p : 7 + 2 * p]).astype(BF16)
            acc += dot(
                jnp.where(px == jcol, one, zero), jnp.where(py == jcol, one, zero), NT
            )
        maps[2, :, 0:NROWS] += acc

    for ref in net_refs:
        if ref.shape[0] == 1:
            chunk(ref, 0)
        else:
            lax.fori_loop(0, ref.shape[0], lambda m, c: (chunk(ref, m), c)[1], 0)
    m = iota((EDGE, LANES), 0)
    lane = iota((EDGE, LANES), 1)
    odd = lax.axis_index("strip") % 2
    sel_even = onehot((m < REACH) & (lane == m + (span - 2) * (1 - odd)))
    sel_odd = onehot((m < REACH) & (lane == m + (span - 2) * odd))
    side = jnp.concatenate(side_columns(even_ref, odd_ref, span), axis=0)
    side = jnp.concatenate([side, jnp.zeros((side.shape[0], LANES - span), BF16)], axis=1)
    feat = maps[...].reshape(3 * JCOLS, LANES).astype(BF16)
    n = 3 * JCOLS
    for sel, out in ((sel_even, to_even), (sel_odd, to_odd)):
        out[:, 0:n] = dot(sel, feat, NT).astype(BF16)
        out[:, n:] = dot(sel, side, NT).astype(BF16)


def network_body(
    pins, n_nets, *refs
):
    net_refs = refs[:n_nets]
    (
        maps, from_even, from_odd, cot, cot_even, cot_odd, even_ref, odd_ref,
        fwd, bwd, first_fwd, first_bwd, bias1, bias2,
    ) = refs[n_nets : 14 + n_nets]
    rest = refs[14 + n_nets :]
    congestion = rest[0]
    grads = rest[1 : 1 + n_nets]
    cotx, feats, back_h, hid, back_p, grad_maps = rest[1 + n_nets :]
    chans = bias1.shape[1]
    span = cot.shape[1]
    cols = cot.shape[0] // chans
    col0, row0 = block_origin(cols, span)
    all_cols = cols * lax.axis_size("col")
    all_rows = span * lax.axis_size("strip")
    strip = lax.axis_index("strip")
    odd = strip % 2
    has_above = (strip > 0).astype(jnp.int32)
    has_below = (strip < lax.axis_size("strip") - 1).astype(jnp.int32)
    left_cols, right_cols = side_columns(even_ref, odd_ref, span)
    n = 3 * JCOLS

    e = jnp.concatenate([from_even[...], from_odd[...]], axis=0)
    m = iota((2 * EDGE, LANES), 0)
    lane = iota((2 * EDGE, LANES), 1)
    k = m % EDGE
    below = (m // EDGE == odd) & (has_below == 1)
    above = (m // EDGE != odd) & (has_above == 1)
    place = onehot(
        (above & (k < REACH) & (lane == (k - 2) % LANES))
        | (below & (k < REACH) & (lane == span + k))
    )
    side_place = onehot(
        (above & (k < 2) & (lane == (k - 2) % LANES))
        | (below & (k < REACH) & (lane == span + k))
    )
    total = maps[...].reshape(n, LANES) + dot(e[:, 0:n], place, TN)
    total = total.astype(BF16).astype(F32).reshape(3, JCOLS, LANES)
    feats[1] = total
    feats[0] = pltpu.roll(total, 1, 2)
    feats[2] = pltpu.roll(total, LANES - 1, 2)

    place2 = side_place[:, span:]
    first_row = 2 * chans
    cotx[first_row : first_row + cols * chans, 0:span] = cot[...]
    step = 512
    for k in range(cols * chans // step):
        s = slice(step * k, step * (k + 1))
        ends = jnp.concatenate([cot_even[:, s], cot_odd[:, s]], axis=0)
        cotx[first_row + step * k : first_row + step * (k + 1), span:LANES] = dot(
            ends, place2, TN
        ).astype(BF16)
    edge_place = dot(e[:, n:], side_place, TN).astype(BF16)
    tail = first_row + cols * chans
    cotx[0:first_row, 0:span] = left_cols
    cotx[0:first_row, span:LANES] = edge_place[0:first_row, span:LANES]
    cotx[tail : tail + first_row, 0:span] = right_cols
    cotx[tail : tail + first_row, span:LANES] = edge_place[first_row : 2 * first_row, span:LANES]
    cotx[tail + first_row :, :] = jnp.zeros((cotx.shape[0] - tail - first_row, LANES), BF16)

    block = GROUP * chans
    window = WINDOW * chans
    groups = pl.cdiv(cols + 2, GROUP)
    back_h[groups * block :, :] = jnp.zeros((back_h.shape[0] - groups * block, LANES), F32)

    def step_a(g, carry):
        lo = pl.multiple_of(g * block, block)
        p = dot(bwd[...], cotx[pl.ds(lo, window), :])
        back_h[pl.ds(lo, block), :] = (
            p[block : 2 * block]
            + pltpu.roll(p[0:block], LANES - 1, 1)
            + pltpu.roll(p[2 * block :], 1, 1)
        )
        return carry

    lax.fori_loop(0, groups, step_a, 0, unroll=True)

    lanes1 = iota((1, LANES), 1)
    row_of = jnp.where(lanes1 < LANES - 64, lanes1, lanes1 - LANES)
    grow = row_of + row0
    row_ok = (row_of >= -1) & (row_of < span + BOX) & (grow >= 0) & (grow < all_rows)
    bias_col = bias1[...].T
    bias_rep = jnp.concatenate([bias_col] * 8, axis=0)
    jo_rows = iota((8 * chans, 1), 0) // chans

    def step_b(g, carry):
        lo8 = pl.multiple_of(g * 8, 8)
        pre = bias_rep
        for r in range(3):
            f = feats[r, :, pl.ds(lo8, 16), :].reshape(3 * 16, LANES).astype(BF16)
            pre = pre + dot(first_fwd[r], f)
        lo = pl.multiple_of(g * 8 * chans, 8 * chans)
        slot = 8 * g + 1 + jo_rows
        gcol = slot - 2 + col0
        col_ok = (slot <= cols + 2) & (gcol >= 0) & (gcol < all_cols)
        ok = col_ok & row_ok
        s = 0.5 + 0.5 * jnp.tanh(0.5 * pre)
        h = pre * s
        slope = s + h * (1.0 - s)
        bh = back_h[pl.ds(lo, 8 * chans), :]
        hid[pl.ds(lo, 8 * chans), :] = jnp.where(ok, h, 0.0).astype(BF16)
        back_p[pl.ds(lo, 8 * chans), :] = jnp.where(ok, bh * slope, 0.0).astype(BF16)
        return carry

    lax.fori_loop(0, pl.cdiv(cols + 2, 8), step_b, 0, unroll=True)

    bias_out = jnp.concatenate([bias2[...].T] * GROUP, axis=0)
    groups_c = pl.cdiv(cols, GROUP)

    def back(g, lo):
        q = dot(first_bwd[...].astype(BF16), back_p[pl.ds(lo, window), :])
        gm = q[16:32] + pltpu.roll(q[0:16], LANES - 1, 1) + pltpu.roll(q[32:48], 1, 1)
        grad_maps[pl.ds(pl.multiple_of(16 * g, 16), 16), :] = gm.astype(BF16)

    def conv(lo):
        p = dot(fwd[...], hid[pl.ds(lo, window), :])
        out = (
            p[block : 2 * block]
            + pltpu.roll(p[0:block], 1, 1)
            + pltpu.roll(p[2 * block :], LANES - 1, 1)
        )
        return (out[:, 0:span] + bias_out).astype(BF16)

    def step_c(g, carry):
        lo = pl.multiple_of(g * block, block)
        congestion[pl.ds(lo, block), :] = conv(lo)
        back(g, lo)
        return carry

    full = cols // GROUP
    lax.fori_loop(0, full, step_c, 0, unroll=True)
    if groups_c > full:
        lo = full * block
        last = (cols - full * GROUP) * chans
        congestion[lo : lo + last, :] = conv(lo)[0:last]
        back(full, lo)

    x_rows = iota((8 * groups_c, 1), 0)
    slot = GROUP * (x_rows // 8) + x_rows % 8 + 2
    slot = jnp.where((x_rows % 8 < GROUP) & (slot < cols + 2), slot, 512).astype(F32)
    nets = net_refs[0].shape[2]
    fcol = col0.astype(F32)
    frow = row0.astype(F32)
    rows = iota((NROWS, nets), 0).astype(F32).astype(BF16)
    one = jnp.ones((), BF16)
    zero = jnp.zeros((), BF16)

    def net_chunk(ref, out, k):
        f, x, y = relative(ref, k, fcol, frow)
        y0, y1 = y(f[2:3]).astype(BF16), y(f[3:4]).astype(BF16)
        in_row = jnp.where((y0 <= rows) & (rows <= y1), one, zero)
        h = dot(grad_maps[:, 0:NROWS], in_row).reshape(groups_c, 2, 8, nets)
        x0, x1 = x(f[0:1]), x(f[1:2])
        in_col = ((x0 <= slot) & (slot <= x1)).reshape(groups_c, 8, nets)
        s0 = jnp.sum(jnp.sum(jnp.where(in_col, h[:, 0], 0.0), axis=0), axis=0, keepdims=True)
        s1 = jnp.sum(jnp.sum(jnp.where(in_col, h[:, 1], 0.0), axis=0), axis=0, keepdims=True)
        out[k, 0:1, :] = s0 / (f[3:4] - f[2:3] + 1.0) + s1 / (f[1:2] - f[0:1] + 1.0)

    for ref, out in zip(net_refs, grads):
        if ref.shape[0] == 1:
            net_chunk(ref, out, 0)
        else:
            lax.fori_loop(0, ref.shape[0], lambda k, c: (net_chunk(ref, out, k), c)[1], 0)


def shards(
    net_box, net_weight, pin_bin, conv_first, bias_first, conv_second, bias_second, cotangent
):
    cols, chans, span = cotangent.shape
    nets, pins = pin_bin.shape[:2]
    strips = lax.axis_size("strip")
    ncol = lax.axis_size("col")
    cot = cotangent.reshape(cols * chans, span)
    edge = 2 * chans
    one_block = pl.BlockSpec((edge, span), lambda i: (0, 0))
    last_block = pl.BlockSpec((edge, span), lambda i: (cols * chans // edge - 1, 0))

    def full(*shape):
        return pl.BlockSpec(shape, lambda i: (0,) * len(shape))

    to_even, to_odd, plain = pl.pallas_call(
        functools.partial(pack_body, pins),
        grid=(1,),
        in_specs=[full(4, nets), full(1, nets), full(pins, 2, nets), one_block, last_block],
        out_specs=[full(FIELDS + 8, nets), full(FIELDS + 8, nets), full(FIELDS, nets)],
        out_shape=[
            jax.ShapeDtypeStruct((FIELDS + 8, nets), F32),
            jax.ShapeDtypeStruct((FIELDS + 8, nets), F32),
            jax.ShapeDtypeStruct((FIELDS, nets), F32),
        ],
        cost_estimate=cost(10000, 400000),
    )(net_box.T, net_weight.reshape(1, nets), pin_bin.transpose(1, 2, 0), cot, cot)

    def swapped(i, n, phase):
        return (i ^ 1) if phase == 0 else (((i + 1) ^ 1) - 1) % n

    def swap_col(x, phase):
        return lax.ppermute(x, "col", [(i, swapped(i, ncol, phase)) for i in range(ncol)])

    def swap_strip(x, phase):
        pairs = []
        for i in range(strips):
            for c in range(ncol):
                j = swapped(i, strips, phase)
                target = i * ncol + (c ^ 1) if abs(i - j) != 1 else j * ncol + c
                pairs.append((i * ncol + c, target))
        return lax.ppermute(x, ("strip", "col"), pairs)

    few = ncol == 4
    by_even = swap_col(to_even, 0)
    by_odd = swap_col(to_odd, 1)
    opposite = [(i, i ^ 2) for i in range(ncol)]
    if few:
        far = lax.ppermute(plain, "col", opposite)
        groups = [plain[None], by_even[None], by_odd[None], far[None]]
    else:
        groups = [lax.all_gather(plain, "col", axis=0)]
    sides = (by_even[None], by_odd[None])

    cot_to_even, cot_to_odd = call(
        cot_edge_body,
        [
            jax.ShapeDtypeStruct((EDGE, cols * chans), BF16),
            jax.ShapeDtypeStruct((EDGE, cols * chans), BF16),
        ],
        1,
        cost=cost(40000000, 1300000),
    )(cot)
    cot_even = swap_strip(cot_to_even, 0)
    cot_odd = swap_strip(cot_to_odd, 1)

    cin = conv_first.shape[3]
    weights = call(
        weight_body,
        [
            jax.ShapeDtypeStruct((3 * GROUP * chans, WINDOW * chans), BF16),
            jax.ShapeDtypeStruct((3 * GROUP * chans, WINDOW * chans), BF16),
            jax.ShapeDtypeStruct((3, 8 * chans, cin * 16), BF16),
            jax.ShapeDtypeStruct((48, WINDOW * chans), F32),
        ],
        2,
        cost=cost(40000000, 1000000),
    )(
        conv_second.reshape(9, chans, chans),
        conv_first.reshape(9, chans, cin).transpose(0, 2, 1),
    )

    width = 3 * JCOLS + 2 * edge
    maps, edge_even, edge_odd = call(
        functools.partial(raster_body, pins, cols, span, len(groups)),
        [
            jax.ShapeDtypeStruct((3, JCOLS, LANES), F32),
            jax.ShapeDtypeStruct((EDGE, width), BF16),
            jax.ShapeDtypeStruct((EDGE, width), BF16),
        ],
        len(groups) + 2,
        cost=cost(1500000000, 1500000),
    )(*groups, *sides)

    from_even = swap_strip(edge_even, 0)
    from_odd = swap_strip(edge_odd, 1)

    rows_x = (cols + 16) * chans
    outs = call(
        functools.partial(network_body, pins, len(groups)),
        [jax.ShapeDtypeStruct((cols * chans, span), BF16)]
        + [jax.ShapeDtypeStruct((g.shape[0], 1, nets), F32) for g in groups],
        len(groups) + 14,
        scratch=[
            pltpu.VMEM((rows_x, LANES), BF16),
            pltpu.VMEM((3, 3, JCOLS, LANES), F32),
            pltpu.VMEM((rows_x, LANES), F32),
            pltpu.VMEM((rows_x, LANES), BF16),
            pltpu.VMEM((rows_x, LANES), BF16),
            pltpu.VMEM((16 * pl.cdiv(cols, GROUP), LANES), BF16),
        ],
        cost=cost(3000000000, 4000000),
    )(
        *groups, maps, from_even, from_odd, cot, cot_even, cot_odd, *sides, *weights,
        bias_first.reshape(1, chans), bias_second.reshape(1, chans),
    )
    congestion = outs[0].reshape(cols, chans, span)
    if few:
        own, for_even, for_odd, for_far = outs[1:]
        net_grad = (
            own
            + swap_col(for_even, 0)
            + swap_col(for_odd, 1)
            + lax.ppermute(for_far, "col", opposite)
        )
    else:
        net_grad = lax.psum_scatter(outs[1], "col", scatter_dimension=0, tiled=True)
    return congestion, net_grad.reshape(nets)


def solution(mesh):
    placed = (
        P(("strip", "col"), None),
        P(("strip", "col")),
        P(("strip", "col"), None, None),
        P(),
        P(),
        P(),
        P(),
        P("col", None, "strip"),
    )
    return jax.shard_map(
        shards,
        mesh=mesh,
        in_specs=placed,
        out_specs=(P("col", None, "strip"), P(("strip", "col"))),
        check_vma=False,
    )
```

```python
import functools

import jax
import jax.numpy as jnp
from jax import lax
from jax.experimental import pallas as pl
from jax.experimental.pallas import tpu as pltpu
from jax.sharding import PartitionSpec as P

F32 = jnp.float32
BF16 = jnp.bfloat16
BOX = 16
REACH = BOX + 1
LANES = 256
NROWS = 144
JCOLS = 144
FIELDS = 16
GROUP = 6
WINDOW = 8
EDGE = 24
VMEM = 24 * 1024 * 1024

NN = (((1,), (0,)), ((), ()))
NT = (((1,), (1,)), ((), ()))
TN = (((0,), (0,)), ((), ()))


def dot(a, b, dims=NN):
    return lax.dot_general(a, b, dims, preferred_element_type=F32)


def iota(shape, dim):
    return lax.broadcasted_iota(jnp.int32, shape, dim)


def onehot(pred):
    return jnp.where(pred, 1.0, 0.0).astype(BF16)


def call(body, out, n_in, scratch=(), cost=None, in_specs=None):
    whole = pl.BlockSpec(memory_space=pltpu.VMEM)
    outs = jax.tree.map(lambda x: whole, out)
    return pl.pallas_call(
        body,
        out_shape=out,
        in_specs=in_specs or [whole] * n_in,
        out_specs=outs,
        scratch_shapes=list(scratch),
        compiler_params=pltpu.CompilerParams(vmem_limit_bytes=VMEM),
        cost_estimate=cost,
    )


def cost(flops, nbytes):
    return pl.CostEstimate(flops=flops, bytes_accessed=nbytes, transcendentals=0)


def pack_body(pins, box, weight, pin, first, last, to_even, to_odd, plain):
    odd = lax.axis_index("col") % 2 == 1
    span = first.shape[1]
    row0 = lax.axis_index("strip") * span
    nets = box.shape[1]
    x0, x1, y0, y1 = (box[k : k + 1, :] for k in range(4))
    height = (y1 - y0 + 1).astype(F32)
    width = (x1 - x0 + 1).astype(F32)
    rows = [x0 // BOX, x0 % BOX, y0 - row0]
    rows = [v.astype(F32) for v in rows]
    rows += [width, height, weight[...] / height, weight[...] / width]
    for p in range(pins):
        rows += [(pin[p, 0:1, :] - y0).astype(F32), (pin[p, 1:2, :] - x0).astype(F32)]
    rows.append(jnp.zeros((FIELDS - len(rows), nets), F32))
    fields = jnp.concatenate(rows, axis=0).astype(BF16)
    plain[...] = fields
    to_even[0:FIELDS, :] = fields
    to_odd[0:FIELDS, :] = fields
    a, b = first[...].astype(F32), last[...].astype(F32)
    for ref, e in ((to_even, jnp.where(odd, a, b)), (to_odd, jnp.where(odd, b, a))):
        for k in range(8):
            ref[FIELDS : FIELDS + 8, span * k : span * (k + 1)] = e[8 * k : 8 * k + 8, :].astype(BF16)


def cot_edge_body(cot, to_even, to_odd):
    odd = lax.axis_index("strip") % 2
    span = cot.shape[1]
    m = iota((2 * EDGE, span), 0)
    lane = iota((2 * EDGE, span), 1)
    up = (m % EDGE < REACH) & (lane == m % EDGE)
    down = (m % EDGE < 2) & (lane == span - 2 + m % EDGE)
    sel = onehot(((m // EDGE == odd) & down) | ((m // EDGE != odd) & up))
    step = 512
    for k in range(cot.shape[0] // step):
        got = dot(sel, cot[step * k : step * (k + 1), :], NT).astype(BF16)
        to_even[:, step * k : step * (k + 1)] = got[:EDGE]
        to_odd[:, step * k : step * (k + 1)] = got[EDGE:]


def block_origin(cols, span):
    return lax.axis_index("col") * cols, lax.axis_index("strip") * span


def side_columns(even_ref, odd_ref, span):
    c = lax.axis_index("col")
    odd = c % 2 == 1

    def unpack(ref):
        e = ref[0, FIELDS : FIELDS + 8, :].astype(F32)
        return jnp.concatenate([e[:, span * k : span * (k + 1)] for k in range(8)], axis=0)

    a, b = unpack(even_ref), unpack(odd_ref)
    left = jnp.where(c > 0, jnp.where(odd, a, b), 0.0)
    right = jnp.where(c < lax.axis_size("col") - 1, jnp.where(odd, b, a), 0.0)
    return left.astype(BF16), right.astype(BF16)


def weight_body(second, first, fwd, bwd, first_fwd, first_bwd):
    chans = second.shape[1]
    tile = onehot(iota((chans, WINDOW * chans), 1) % chans == iota((chans, WINDOW * chans), 0))
    lane_t = iota((chans, WINDOW * chans), 1) // chans
    cin = first.shape[1]
    ftile = onehot(iota((cin, cin * 16), 1) // 16 == iota((cin, cin * 16), 0))
    ft = iota((chans, cin * 16), 1) % 16
    row8 = iota((8, WINDOW * chans), 0)
    lane8 = iota((8, WINDOW * chans), 1) // chans
    for r in range(3):
        taps = [dot(second[3 * r + c], tile) for c in range(3)]
        flipped = [dot(second[3 * r + c], tile, TN) for c in range(3)]
        for jo in range(GROUP):
            lo = (r * GROUP + jo) * chans
            acc = jnp.zeros((chans, WINDOW * chans), F32)
            acc2 = acc
            for c in range(3):
                acc = jnp.where(lane_t == jo + c, taps[c], acc)
                acc2 = jnp.where(lane_t == jo + 2 - c, flipped[c], acc2)
            fwd[lo : lo + chans, :] = acc.astype(BF16)
            bwd[lo : lo + chans, :] = acc2.astype(BF16)
        ftaps = [dot(first[3 * r + c], ftile, TN) for c in range(3)]
        parts = []
        for jo in range(8):
            acc = jnp.zeros((chans, cin * 16), F32)
            for c in range(3):
                acc = jnp.where(ft == jo + c, ftaps[c], acc)
            parts.append(acc)
        first_fwd[r] = jnp.concatenate(parts, axis=0).astype(BF16)
        fback = [dot(first[3 * r + c], tile) for c in range(3)]
        for ch in range(2):
            acc = jnp.zeros((8, WINDOW * chans), F32)
            for c in range(3):
                row = jnp.broadcast_to(fback[c][ch : ch + 1, :], acc.shape)
                acc = jnp.where((lane8 == row8 + 2 - c) & (row8 < GROUP), row, acc)
            first_bwd[16 * r + 8 * ch : 16 * r + 8 * ch + 8, :] = acc


def spread(p, block):
    lane = iota((block, p.shape[1]), 1)
    low = pltpu.roll(p[0:block], p.shape[1] - 1, 1)
    high = pltpu.roll(p[2 * block :], 1, 1)
    last = lane == p.shape[1] - 1
    first = lane == 0
    same = p[block : 2 * block] + jnp.where(last, 0.0, low) + jnp.where(first, 0.0, high)
    return same, jnp.where(last, low, 0.0) + jnp.where(first, high, 0.0)


def window_of(ref, g, cols, chans):
    lo, hi = (GROUP * g - 2) * chans, (GROUP * g - 2 + WINDOW) * chans
    top = cols * chans
    parts = []
    if lo < 0:
        parts.append(jnp.zeros((-lo, ref.shape[1]), BF16))
    parts.append(ref[max(lo, 0) : min(hi, top), :])
    if hi > top:
        parts.append(jnp.zeros((hi - top, ref.shape[1]), BF16))
    return parts[0] if len(parts) == 1 else jnp.concatenate(parts, axis=0)


def back_own_body(chans, cot, bwd, same_ref, other_ref):
    cols = cot.shape[0] // chans
    block = GROUP * chans
    w = bwd[...]
    for g in range(pl.cdiv(cols + 2, GROUP)):
        same, other = spread(dot(w, window_of(cot, g, cols, chans)), block)
        same_ref[block * g : block * (g + 1), :] = same
        other_ref[block * g : block * (g + 1), :] = other


def halo_place(span):
    strip = lax.axis_index("strip")
    odd = strip % 2
    has_above = (strip > 0).astype(jnp.int32)
    has_below = (strip < lax.axis_size("strip") - 1).astype(jnp.int32)
    m = iota((2 * EDGE, LANES), 0)
    lane = iota((2 * EDGE, LANES), 1)
    k = m % EDGE
    below = (m // EDGE == odd) & (has_below == 1) & (k < REACH) & (lane == span + k)
    above = (m // EDGE != odd) & (has_above == 1) & (lane == (k - 2) % LANES)
    return onehot((above & (k < REACH)) | below), onehot((above & (k < 2)) | below)


def back_halo_body(chans, cot_even, cot_odd, bwd, same_ref, other_ref, back_h, halo):
    cols = cot_even.shape[1] // chans
    span = same_ref.shape[1]
    place = halo_place(span)[1][:, span:]
    step = 512
    for k in range(cols * chans // step):
        s = slice(step * k, step * (k + 1))
        ends = jnp.concatenate([cot_even[:, s], cot_odd[:, s]], axis=0)
        halo[s, :] = dot(ends, place, TN).astype(BF16)
    block = GROUP * chans
    w = bwd[...]
    for g in range(pl.cdiv(cols + 2, GROUP)):
        same, other = spread(dot(w, window_of(halo, g, cols, chans)), block)
        rows = slice(block * g, block * (g + 1))
        back_h[rows, 0:span] = same_ref[rows, :] + other
        back_h[rows, span:] = same + other_ref[rows, :]


def relative(ref, m, col0):
    f = ref[m, 0:FIELDS, :].astype(F32)
    x = f[0:1] * float(BOX) + f[1:2] - (col0 - 2.0)
    y = f[2:3]
    width, height = f[3:4], f[4:5]
    cut = lambda v: jnp.clip(v, -2.0, 250.0)
    return f, x, y, cut(x), cut(x + width - 1.0), y + height - 1.0, width, height, cut


def raster_body(pins, cols, span, n_nets, *refs):
    net_refs = refs[:n_nets]
    even_ref, odd_ref, maps, to_even, to_odd = refs[n_nets:]
    col0 = block_origin(cols, span)[0].astype(F32)
    maps[...] = jnp.zeros_like(maps)
    nets = net_refs[0].shape[2]
    step = nets
    jcol = iota((JCOLS, step), 0).astype(F32).astype(BF16)
    one = jnp.ones((), BF16)
    zero = jnp.zeros((), BF16)

    def chunk(ref, m):
        f, x, y, x0, x1, y1, width, height, cut = relative(ref, m, col0)
        x0, x1, y0, y1 = x0.astype(BF16), x1.astype(BF16), y.astype(BF16), y1.astype(BF16)
        vh, vv = f[5:6].astype(BF16), f[6:7].astype(BF16)
        in_col = (x0 <= jcol) & (jcol <= x1)
        in_row = jnp.where((y0 <= jcol) & (jcol <= y1), one, zero)
        maps[0, :, 0:NROWS] += dot(jnp.where(in_col, vh, zero), in_row, NT)
        maps[1, :, 0:NROWS] += dot(jnp.where(in_col, vv, zero), in_row, NT)
        acc = jnp.zeros((JCOLS, NROWS), F32)
        for p in range(pins):
            py = (y + f[7 + 2 * p : 8 + 2 * p]).astype(BF16)
            px = cut(x + f[8 + 2 * p : 9 + 2 * p]).astype(BF16)
            acc += dot(
                jnp.where(px == jcol, one, zero), jnp.where(py == jcol, one, zero), NT
            )
        maps[2, :, 0:NROWS] += acc

    for ref in net_refs:
        if ref.shape[0] == 1:
            chunk(ref, 0)
        else:
            lax.fori_loop(0, ref.shape[0], lambda m, c: (chunk(ref, m), c)[1], 0)
    m = iota((EDGE, LANES), 0)
    lane = iota((EDGE, LANES), 1)
    odd = lax.axis_index("strip") % 2
    sel_even = onehot((m < REACH) & (lane == m + (span - 2) * (1 - odd)))
    sel_odd = onehot((m < REACH) & (lane == m + (span - 2) * odd))
    side = jnp.concatenate(side_columns(even_ref, odd_ref, span), axis=0)
    side = jnp.concatenate([side, jnp.zeros((side.shape[0], LANES - span), BF16)], axis=1)
    feat = maps[...].reshape(3 * JCOLS, LANES).astype(BF16)
    n = 3 * JCOLS
    for sel, out in ((sel_even, to_even), (sel_odd, to_odd)):
        out[:, 0:n] = dot(sel, feat, NT).astype(BF16)
        out[:, n:] = dot(sel, side, NT).astype(BF16)


def network_body(
    pins, n_nets, *refs
):
    net_refs = refs[:n_nets]
    (
        maps, from_even, from_odd, back_h, even_ref, odd_ref,
        fwd, bwd, first_fwd, first_bwd, bias1, bias2,
    ) = refs[n_nets : 12 + n_nets]
    rest = refs[12 + n_nets :]
    congestion = rest[0]
    grads = rest[1 : 1 + n_nets]
    feats, hid, back_p, grad_maps = rest[1 + n_nets :]
    chans = bias1.shape[1]
    span = congestion.shape[1]
    cols = congestion.shape[0] // chans
    col0, row0 = block_origin(cols, span)
    all_cols = cols * lax.axis_size("col")
    all_rows = span * lax.axis_size("strip")
    left_cols, right_cols = side_columns(even_ref, odd_ref, span)
    n = 3 * JCOLS

    e = jnp.concatenate([from_even[...], from_odd[...]], axis=0)
    place, side_place = halo_place(span)
    total = maps[...].reshape(n, LANES) + dot(e[:, 0:n], place, TN)
    total = total.astype(BF16).astype(F32).reshape(3, JCOLS, LANES)
    feats[1] = total
    feats[0] = pltpu.roll(total, 1, 2)
    feats[2] = pltpu.roll(total, LANES - 1, 2)

    edge = 2 * chans
    block = GROUP * chans
    window = WINDOW * chans
    outer = dot(e[:, n:], side_place, TN).astype(BF16)
    fixes = []
    for k, main in enumerate((left_cols, right_cols)):
        ext = jnp.concatenate([main, outer[edge * k : edge * (k + 1), span:]], axis=1)
        taps = jnp.concatenate(
            [bwd[block * r : block * r + edge, edge * k : edge * (k + 1)] for r in range(3)], axis=0
        )
        p = dot(taps, ext)
        fixes.append(
            p[edge : 2 * edge]
            + pltpu.roll(p[0:edge], LANES - 1, 1)
            + pltpu.roll(p[2 * edge :], 1, 1)
        )

    lanes1 = iota((1, LANES), 1)
    row_of = jnp.where(lanes1 < LANES - 64, lanes1, lanes1 - LANES)
    grow = row_of + row0
    row_ok = (row_of >= -1) & (row_of < span + BOX) & (grow >= 0) & (grow < all_rows)
    bias_col = bias1[...].T
    bias_rep = jnp.concatenate([bias_col] * 8, axis=0)
    jo_rows = iota((8 * chans, 1), 0) // chans

    def step_b(g):
        lo8 = g * 8
        pre = bias_rep
        for r in range(3):
            f = feats[r, :, pl.ds(lo8, 16), :].reshape(3 * 16, LANES).astype(BF16)
            pre = pre + dot(first_fwd[r], f)
        lo = g * 8 * chans
        slot = 8 * g + 1 + jo_rows
        gcol = slot - 2 + col0
        col_ok = (slot <= cols + 2) & (gcol >= 0) & (gcol < all_cols)
        ok = col_ok & row_ok
        s = 0.5 + 0.5 * jnp.tanh(0.5 * pre)
        h = pre * s
        slope = s + h * (1.0 - s)
        bh = back_h[pl.ds(lo, 8 * chans), :]
        if g in (0, cols // 8):
            fix = fixes[0 if g == 0 else 1]
            bh = jnp.concatenate([bh[0:edge] + fix, bh[edge:]], axis=0)
        hid[pl.ds(lo, 8 * chans), :] = jnp.where(ok, h, 0.0).astype(BF16)
        back_p[pl.ds(lo, 8 * chans), :] = jnp.where(ok, bh * slope, 0.0).astype(BF16)

    for g in range(pl.cdiv(cols + 2, 8)):
        step_b(g)

    bias_out = jnp.concatenate([bias2[...].T] * GROUP, axis=0)
    groups_c = pl.cdiv(cols, GROUP)

    def back(g, lo):
        q = dot(first_bwd[...].astype(BF16), back_p[pl.ds(lo, window), :])
        gm = q[16:32] + pltpu.roll(q[0:16], LANES - 1, 1) + pltpu.roll(q[32:48], 1, 1)
        grad_maps[pl.ds(pl.multiple_of(16 * g, 16), 16), :] = gm.astype(BF16)

    def conv(lo):
        p = dot(fwd[...], hid[pl.ds(lo, window), :])
        out = (
            p[block : 2 * block]
            + pltpu.roll(p[0:block], 1, 1)
            + pltpu.roll(p[2 * block :], LANES - 1, 1)
        )
        return (out[:, 0:span] + bias_out).astype(BF16)

    def step_c(g, carry):
        lo = pl.multiple_of(g * block, block)
        congestion[pl.ds(lo, block), :] = conv(lo)
        back(g, lo)
        return carry

    full = cols // GROUP
    lax.fori_loop(0, full, step_c, 0, unroll=True)
    if groups_c > full:
        lo = full * block
        last = (cols - full * GROUP) * chans
        congestion[lo : lo + last, :] = conv(lo)[0:last]
        back(full, lo)

    x_rows = iota((8 * groups_c, 1), 0)
    slot = GROUP * (x_rows // 8) + x_rows % 8 + 2
    slot = jnp.where((x_rows % 8 < GROUP) & (slot < cols + 2), slot, 512).astype(F32)
    nets = net_refs[0].shape[2]
    fcol = col0.astype(F32)
    rows = iota((NROWS, nets), 0).astype(F32).astype(BF16)
    one = jnp.ones((), BF16)
    zero = jnp.zeros((), BF16)

    def net_chunk(ref, out, k):
        f, x, y, x0, x1, y1, width, height, cut = relative(ref, k, fcol)
        y0, y1 = y.astype(BF16), y1.astype(BF16)
        in_row = jnp.where((y0 <= rows) & (rows <= y1), one, zero)
        h = dot(grad_maps[:, 0:NROWS], in_row).reshape(groups_c, 2, 8, nets)
        in_col = ((x0 <= slot) & (slot <= x1)).reshape(groups_c, 8, nets)
        s0 = jnp.sum(jnp.sum(jnp.where(in_col, h[:, 0], 0.0), axis=0), axis=0, keepdims=True)
        s1 = jnp.sum(jnp.sum(jnp.where(in_col, h[:, 1], 0.0), axis=0), axis=0, keepdims=True)
        out[k, 0:1, :] = s0 / height + s1 / width

    for ref, out in zip(net_refs, grads):
        if ref.shape[0] == 1:
            net_chunk(ref, out, 0)
        else:
            lax.fori_loop(0, ref.shape[0], lambda k, c: (net_chunk(ref, out, k), c)[1], 0)


def shards(
    net_box, net_weight, pin_bin, conv_first, bias_first, conv_second, bias_second, cotangent
):
    cols, chans, span = cotangent.shape
    nets, pins = pin_bin.shape[:2]
    strips = lax.axis_size("strip")
    ncol = lax.axis_size("col")
    cot = cotangent.reshape(cols * chans, span)
    edge = 2 * chans
    one_block = pl.BlockSpec((edge, span), lambda i: (0, 0))
    last_block = pl.BlockSpec((edge, span), lambda i: (cols * chans // edge - 1, 0))

    def full(*shape):
        return pl.BlockSpec(shape, lambda i: (0,) * len(shape))

    to_even, to_odd, plain = pl.pallas_call(
        functools.partial(pack_body, pins),
        grid=(1,),
        in_specs=[full(4, nets), full(1, nets), full(pins, 2, nets), one_block, last_block],
        out_specs=[full(FIELDS + 8, nets), full(FIELDS + 8, nets), full(FIELDS, nets)],
        out_shape=[
            jax.ShapeDtypeStruct((FIELDS + 8, nets), BF16),
            jax.ShapeDtypeStruct((FIELDS + 8, nets), BF16),
            jax.ShapeDtypeStruct((FIELDS, nets), BF16),
        ],
        cost_estimate=cost(10000, 400000),
    )(net_box.T, net_weight.reshape(1, nets), pin_bin.transpose(1, 2, 0), cot, cot)

    def swapped(i, n, phase):
        return (i ^ 1) if phase == 0 else (((i + 1) ^ 1) - 1) % n

    def swap_col(x, phase):
        return lax.ppermute(x, "col", [(i, swapped(i, ncol, phase)) for i in range(ncol)])

    def swap_strip(x, phase):
        pairs = []
        for i in range(strips):
            for c in range(ncol):
                j = swapped(i, strips, phase)
                target = i * ncol + (c ^ 1) if abs(i - j) != 1 else j * ncol + c
                pairs.append((i * ncol + c, target))
        return lax.ppermute(x, ("strip", "col"), pairs)

    few = ncol == 4
    by_even = swap_col(to_even, 0)
    by_odd = swap_col(to_odd, 1)
    opposite = [(i, i ^ 2) for i in range(ncol)]
    if few:
        far = lax.ppermute(plain, "col", opposite)
        groups = [plain[None], by_even[None], by_odd[None], far[None]]
    else:
        groups = [lax.all_gather(plain, "col", axis=0)]
    sides = (by_even[None], by_odd[None])

    cot_to_even, cot_to_odd = call(
        cot_edge_body,
        [
            jax.ShapeDtypeStruct((EDGE, cols * chans), BF16),
            jax.ShapeDtypeStruct((EDGE, cols * chans), BF16),
        ],
        1,
        cost=cost(40000000, 1300000),
    )(lax.optimization_barrier((cot, plain))[0])
    cot_even = swap_strip(cot_to_even, 0)
    cot_odd = swap_strip(cot_to_odd, 1)

    cin = conv_first.shape[3]
    weights = call(
        weight_body,
        [
            jax.ShapeDtypeStruct((3 * GROUP * chans, WINDOW * chans), BF16),
            jax.ShapeDtypeStruct((3 * GROUP * chans, WINDOW * chans), BF16),
            jax.ShapeDtypeStruct((3, 8 * chans, cin * 16), BF16),
            jax.ShapeDtypeStruct((48, WINDOW * chans), F32),
        ],
        2,
        cost=cost(40000000, 1000000),
    )(
        conv_second.reshape(9, chans, chans),
        conv_first.reshape(9, chans, cin).transpose(0, 2, 1),
    )

    hidden_rows = GROUP * pl.cdiv(cols + 2, GROUP) * chans
    own = call(
        functools.partial(back_own_body, chans),
        [jax.ShapeDtypeStruct((hidden_rows, span), F32)] * 2,
        2,
        cost=cost(2000000000, 1000000),
    )(cot, weights[1])
    width = 3 * JCOLS + 2 * edge
    maps, edge_even, edge_odd = call(
        functools.partial(raster_body, pins, cols, span, len(groups)),
        [
            jax.ShapeDtypeStruct((3, JCOLS, LANES), F32),
            jax.ShapeDtypeStruct((EDGE, width), BF16),
            jax.ShapeDtypeStruct((EDGE, width), BF16),
        ],
        len(groups) + 2,
        cost=cost(1500000000, 1500000),
    )(*groups, *sides)

    from_even = swap_strip(edge_even, 0)
    from_odd = swap_strip(edge_odd, 1)

    rows_x = 8 * pl.cdiv(cols + 2, 8) * chans
    back_h = call(
        functools.partial(back_halo_body, chans),
        jax.ShapeDtypeStruct((rows_x, LANES), F32),
        5,
        scratch=[pltpu.VMEM((cols * chans, span), BF16)],
        cost=cost(2000000000, 1000000),
    )(cot_even, cot_odd, weights[1], *own)

    outs = call(
        functools.partial(network_body, pins, len(groups)),
        [jax.ShapeDtypeStruct((cols * chans, span), BF16)]
        + [jax.ShapeDtypeStruct((g.shape[0], 1, nets), F32) for g in groups],
        len(groups) + 12,
        scratch=[
            pltpu.VMEM((3, 3, JCOLS, LANES), F32),
            pltpu.VMEM((rows_x, LANES), BF16),
            pltpu.VMEM((rows_x, LANES), BF16),
            pltpu.VMEM((16 * pl.cdiv(cols, GROUP), LANES), BF16),
        ],
        cost=cost(3000000000, 4000000),
    )(
        *groups, maps, from_even, from_odd, back_h, *sides, *weights,
        bias_first.reshape(1, chans), bias_second.reshape(1, chans),
    )
    congestion = outs[0].reshape(cols, chans, span)
    if few:
        own, for_even, for_odd, for_far = outs[1:]
        net_grad = (
            own
            + swap_col(for_even, 0)
            + swap_col(for_odd, 1)
            + lax.ppermute(for_far, "col", opposite)
        )
    else:
        net_grad = lax.psum_scatter(outs[1], "col", scatter_dimension=0, tiled=True)
    return congestion, net_grad.reshape(nets)


def solution(mesh):
    placed = (
        P(("strip", "col"), None),
        P(("strip", "col")),
        P(("strip", "col"), None, None),
        P(),
        P(),
        P(),
        P(),
        P("col", None, "strip"),
    )
    return jax.shard_map(
        shards,
        mesh=mesh,
        in_specs=placed,
        out_specs=(P("col", None, "strip"), P(("strip", "col"))),
        check_vma=False,
    )
```

```python
import functools

import jax
import jax.numpy as jnp
from jax import lax
from jax.experimental import pallas as pl
from jax.experimental.pallas import tpu as pltpu
from jax.sharding import PartitionSpec as P

F32 = jnp.float32
BF16 = jnp.bfloat16
BOX = 16
REACH = BOX + 1
LANES = 256
NROWS = 144
JCOLS = 144
FIELDS = 16
GROUP = 6
WINDOW = 8
EDGE = 24
VMEM = 24 * 1024 * 1024

NN = (((1,), (0,)), ((), ()))
NT = (((1,), (1,)), ((), ()))
TN = (((0,), (0,)), ((), ()))


def dot(a, b, dims=NN):
    return lax.dot_general(a, b, dims, preferred_element_type=F32)


def iota(shape, dim):
    return lax.broadcasted_iota(jnp.int32, shape, dim)


def onehot(pred):
    return jnp.where(pred, 1.0, 0.0).astype(BF16)


def call(body, out, n_in, scratch=(), cost=None, in_specs=None):
    whole = pl.BlockSpec(memory_space=pltpu.VMEM)
    outs = jax.tree.map(lambda x: whole, out)
    return pl.pallas_call(
        body,
        out_shape=out,
        in_specs=in_specs or [whole] * n_in,
        out_specs=outs,
        scratch_shapes=list(scratch),
        compiler_params=pltpu.CompilerParams(vmem_limit_bytes=VMEM),
        cost_estimate=cost,
    )


def cost(flops, nbytes):
    return pl.CostEstimate(flops=flops, bytes_accessed=nbytes, transcendentals=0)


def pack_body(pins, box, weight, pin, first, last, to_even, to_odd, plain):
    odd = lax.axis_index("col") % 2 == 1
    span = first.shape[1]
    row0 = lax.axis_index("strip") * span
    nets = box.shape[1]
    x0, x1, y0, y1 = (box[k : k + 1, :] for k in range(4))
    height = (y1 - y0 + 1).astype(F32)
    width = (x1 - x0 + 1).astype(F32)
    rows = [x0 // BOX, x0 % BOX, y0 - row0]
    rows = [v.astype(F32) for v in rows]
    rows += [width, height, weight[...] / height, weight[...] / width]
    for p in range(pins):
        rows += [(pin[p, 0:1, :] - y0).astype(F32), (pin[p, 1:2, :] - x0).astype(F32)]
    rows.append(jnp.zeros((FIELDS - len(rows), nets), F32))
    fields = jnp.concatenate(rows, axis=0).astype(BF16)
    plain[...] = fields
    to_even[0:FIELDS, :] = fields
    to_odd[0:FIELDS, :] = fields
    a, b = first[...].astype(F32), last[...].astype(F32)
    for ref, e in ((to_even, jnp.where(odd, a, b)), (to_odd, jnp.where(odd, b, a))):
        for k in range(8):
            ref[FIELDS : FIELDS + 8, span * k : span * (k + 1)] = e[8 * k : 8 * k + 8, :].astype(BF16)


def cot_edge_body(cot, to_even, to_odd):
    odd = lax.axis_index("strip") % 2
    span = cot.shape[1]
    m = iota((2 * EDGE, span), 0)
    lane = iota((2 * EDGE, span), 1)
    up = (m % EDGE < REACH) & (lane == m % EDGE)
    down = (m % EDGE < 2) & (lane == span - 2 + m % EDGE)
    sel = onehot(((m // EDGE == odd) & down) | ((m // EDGE != odd) & up))
    step = 512
    for k in range(cot.shape[0] // step):
        got = dot(sel, cot[step * k : step * (k + 1), :], NT).astype(BF16)
        to_even[:, step * k : step * (k + 1)] = got[:EDGE]
        to_odd[:, step * k : step * (k + 1)] = got[EDGE:]


def block_origin(cols, span):
    return lax.axis_index("col") * cols, lax.axis_index("strip") * span


def side_columns(even_ref, odd_ref, span):
    c = lax.axis_index("col")
    odd = c % 2 == 1

    def unpack(ref):
        e = ref[0, FIELDS : FIELDS + 8, :].astype(F32)
        return jnp.concatenate([e[:, span * k : span * (k + 1)] for k in range(8)], axis=0)

    a, b = unpack(even_ref), unpack(odd_ref)
    left = jnp.where(c > 0, jnp.where(odd, a, b), 0.0)
    right = jnp.where(c < lax.axis_size("col") - 1, jnp.where(odd, b, a), 0.0)
    return left.astype(BF16), right.astype(BF16)


def weight_body(second, first, fwd, bwd, first_fwd, first_bwd):
    chans = second.shape[1]
    tile = onehot(iota((chans, WINDOW * chans), 1) % chans == iota((chans, WINDOW * chans), 0))
    lane_t = iota((chans, WINDOW * chans), 1) // chans
    cin = first.shape[1]
    taps_all = 9 * 16
    ftile = onehot(iota((cin, taps_all), 1) // 16 % cin == iota((cin, taps_all), 0))
    flane = iota((chans, taps_all), 1)
    fparts = [jnp.zeros((chans, taps_all), F32)] * 8
    back_parts = []
    row8 = iota((8, WINDOW * chans), 0)
    lane8 = iota((8, WINDOW * chans), 1) // chans
    for r in range(3):
        taps = [dot(second[3 * r + c], tile) for c in range(3)]
        flipped = [dot(second[3 * r + c], tile, TN) for c in range(3)]
        for jo in range(GROUP):
            lo = (r * GROUP + jo) * chans
            acc = jnp.zeros((chans, WINDOW * chans), F32)
            acc2 = acc
            for c in range(3):
                acc = jnp.where(lane_t == jo + c, taps[c], acc)
                acc2 = jnp.where(lane_t == jo + 2 - c, flipped[c], acc2)
            wide = WINDOW * chans
            fwd[jo * chans : (jo + 1) * chans, r * wide : (r + 1) * wide] = acc.astype(BF16)
            bwd[lo : lo + chans, :] = (0.5 * acc2).astype(BF16)
        ftaps = [dot(first[3 * r + c], ftile, TN) for c in range(3)]
        for jo in range(8):
            for c in range(3):
                hit = (flane // (16 * cin) == r) & (flane % 16 == jo + c)
                fparts[jo] = jnp.where(hit, 0.5 * ftaps[c], fparts[jo])
        fback = [dot(first[3 * r + c], tile) for c in range(3)]
        for ch in range(2):
            acc = jnp.zeros((8, WINDOW * chans), F32)
            for c in range(3):
                row = jnp.broadcast_to(fback[c][ch : ch + 1, :], acc.shape)
                acc = jnp.where((lane8 == row8 + 2 - c) & (row8 < GROUP), row, acc)
            back_parts.append(acc)
    first_fwd[...] = jnp.concatenate(fparts, axis=0).astype(BF16)
    first_bwd[...] = jnp.concatenate(back_parts, axis=0).astype(BF16)


def spread(p, block):
    lane = iota((block, p.shape[1]), 1)
    low = pltpu.roll(p[0:block], p.shape[1] - 1, 1)
    high = pltpu.roll(p[2 * block :], 1, 1)
    last = lane == p.shape[1] - 1
    first = lane == 0
    same = p[block : 2 * block] + jnp.where(last, 0.0, low) + jnp.where(first, 0.0, high)
    return same, jnp.where(last, low, 0.0) + jnp.where(first, high, 0.0)


def window_of(ref, g, cols, chans):
    lo, hi = (GROUP * g - 2) * chans, (GROUP * g - 2 + WINDOW) * chans
    top = cols * chans
    parts = []
    if lo < 0:
        parts.append(jnp.zeros((-lo, ref.shape[1]), BF16))
    parts.append(ref[max(lo, 0) : min(hi, top), :])
    if hi > top:
        parts.append(jnp.zeros((hi - top, ref.shape[1]), BF16))
    return parts[0] if len(parts) == 1 else jnp.concatenate(parts, axis=0)


def back_own_body(chans, cot, bwd, same_ref, other_ref):
    cols = cot.shape[0] // chans
    block = GROUP * chans
    w = bwd[...]
    for g in range(pl.cdiv(cols + 2, GROUP)):
        same, other = spread(dot(w, window_of(cot, g, cols, chans)), block)
        same_ref[block * g : block * (g + 1), :] = same
        other_ref[block * g : block * (g + 1), :] = other


def halo_place(span):
    strip = lax.axis_index("strip")
    odd = strip % 2
    has_above = (strip > 0).astype(jnp.int32)
    has_below = (strip < lax.axis_size("strip") - 1).astype(jnp.int32)
    m = iota((2 * EDGE, LANES), 0)
    lane = iota((2 * EDGE, LANES), 1)
    k = m % EDGE
    below = (m // EDGE == odd) & (has_below == 1) & (k < REACH) & (lane == span + k)
    above = (m // EDGE != odd) & (has_above == 1) & (lane == (k - 2) % LANES)
    return onehot((above & (k < REACH)) | below), onehot((above & (k < 2)) | below)


def back_halo_body(chans, cot_even, cot_odd, bwd, same_ref, other_ref, back_h, halo):
    cols = cot_even.shape[1] // chans
    span = same_ref.shape[1]
    place = halo_place(span)[1][:, span:]
    step = 512
    for k in range(cols * chans // step):
        s = slice(step * k, step * (k + 1))
        ends = jnp.concatenate([cot_even[:, s], cot_odd[:, s]], axis=0)
        halo[s, :] = dot(ends, place, TN).astype(BF16)
    block = GROUP * chans
    w = bwd[...]
    for g in range(pl.cdiv(cols + 2, GROUP)):
        same, other = spread(dot(w, window_of(halo, g, cols, chans)), block)
        rows = slice(block * g, block * (g + 1))
        back_h[rows, 0:span] = same_ref[rows, :] + other
        back_h[rows, span:] = same + other_ref[rows, :]


def relative(ref, m, col0):
    f = ref[m, 0:FIELDS, :].astype(F32)
    x = f[0:1] * float(BOX) + f[1:2] - (col0 - 2.0)
    y = f[2:3]
    width, height = f[3:4], f[4:5]
    cut = lambda v: jnp.clip(v, -2.0, 250.0)
    return f, x, y, cut(x), cut(x + width - 1.0), y + height - 1.0, width, height, cut


def raster_body(pins, cols, span, n_nets, *refs):
    net_refs = refs[:n_nets]
    even_ref, odd_ref, maps, to_even, to_odd = refs[n_nets:]
    col0 = block_origin(cols, span)[0].astype(F32)
    maps[...] = jnp.zeros_like(maps)
    nets = net_refs[0].shape[2]
    step = nets
    jcol = iota((JCOLS, step), 0).astype(F32).astype(BF16)
    one = jnp.ones((), BF16)
    zero = jnp.zeros((), BF16)

    def chunk(ref, m):
        f, x, y, x0, x1, y1, width, height, cut = relative(ref, m, col0)
        x0, x1, y0, y1 = x0.astype(BF16), x1.astype(BF16), y.astype(BF16), y1.astype(BF16)
        vh, vv = f[5:6].astype(BF16), f[6:7].astype(BF16)
        in_col = (x0 <= jcol) & (jcol <= x1)
        in_row = jnp.where((y0 <= jcol) & (jcol <= y1), one, zero)
        demand = jnp.concatenate(
            [jnp.where(in_col, vh, zero), jnp.where(in_col, vv, zero)], axis=0
        )
        got = dot(demand, in_row, NT)
        pin_cols, pin_rows = [], []
        for p in range(pins):
            py = (y + f[7 + 2 * p : 8 + 2 * p]).astype(BF16)
            px = cut(x + f[8 + 2 * p : 9 + 2 * p]).astype(BF16)
            pin_cols.append(jnp.where(px == jcol, one, zero))
            pin_rows.append(jnp.where(py == jcol, one, zero))
        pinned = dot(
            jnp.concatenate(pin_cols, axis=1), jnp.concatenate(pin_rows, axis=1), NT
        )
        maps[0, :, 0:NROWS] += got[0:JCOLS]
        maps[1, :, 0:NROWS] += got[JCOLS:]
        maps[2, :, 0:NROWS] += pinned

    for ref in net_refs:
        if ref.shape[0] == 1:
            chunk(ref, 0)
        else:
            lax.fori_loop(0, ref.shape[0], lambda m, c: (chunk(ref, m), c)[1], 0)
    m = iota((EDGE, LANES), 0)
    lane = iota((EDGE, LANES), 1)
    odd = lax.axis_index("strip") % 2
    sel_even = onehot((m < REACH) & (lane == m + (span - 2) * (1 - odd)))
    sel_odd = onehot((m < REACH) & (lane == m + (span - 2) * odd))
    side = jnp.concatenate(side_columns(even_ref, odd_ref, span), axis=0)
    side = jnp.concatenate([side, jnp.zeros((side.shape[0], LANES - span), BF16)], axis=1)
    feat = maps[...].reshape(3 * JCOLS, LANES).astype(BF16)
    n = 3 * JCOLS
    for sel, out in ((sel_even, to_even), (sel_odd, to_odd)):
        out[:, 0:n] = dot(sel, feat, NT).astype(BF16)
        out[:, n:] = dot(sel, side, NT).astype(BF16)


def network_body(
    pins, n_nets, *refs
):
    net_refs = refs[:n_nets]
    (
        maps, from_even, from_odd, back_h, even_ref, odd_ref,
        fwd, bwd, first_fwd, first_bwd, bias1, bias2,
    ) = refs[n_nets : 12 + n_nets]
    rest = refs[12 + n_nets :]
    congestion = rest[0]
    grads = rest[1 : 1 + n_nets]
    feats, hid, back_p, grad_maps = rest[1 + n_nets :]
    chans = bias1.shape[1]
    span = congestion.shape[1]
    cols = congestion.shape[0] // chans
    col0, row0 = block_origin(cols, span)
    all_cols = cols * lax.axis_size("col")
    all_rows = span * lax.axis_size("strip")
    left_cols, right_cols = side_columns(even_ref, odd_ref, span)
    n = 3 * JCOLS

    e = jnp.concatenate([from_even[...], from_odd[...]], axis=0)
    place, side_place = halo_place(span)
    total = maps[...].reshape(n, LANES) + dot(e[:, 0:n], place, TN)
    total = total.astype(BF16).astype(F32).reshape(3, JCOLS, LANES)
    feats[1] = total
    feats[0] = pltpu.roll(total, 1, 2)
    feats[2] = pltpu.roll(total, LANES - 1, 2)

    edge = 2 * chans
    block = GROUP * chans
    window = WINDOW * chans
    outer = dot(e[:, n:], side_place, TN).astype(BF16)
    fixes = []
    for k, main in enumerate((left_cols, right_cols)):
        ext = jnp.concatenate([main, outer[edge * k : edge * (k + 1), span:]], axis=1)
        taps = jnp.concatenate(
            [bwd[block * r : block * r + edge, edge * k : edge * (k + 1)] for r in range(3)], axis=0
        )
        p = dot(taps, ext)
        fixes.append(
            p[edge : 2 * edge]
            + pltpu.roll(p[0:edge], LANES - 1, 1)
            + pltpu.roll(p[2 * edge :], 1, 1)
        )

    lanes1 = iota((1, span), 1)
    grow = jnp.where(lanes1 < BOX, lanes1 + span, lanes1 - span) + row0
    used = (lanes1 < BOX) | (lanes1 == span - 1)
    row_ok = used & (grow >= 0) & (grow < all_rows)
    bias_half = jnp.concatenate([0.5 * bias1[...].T] * 8, axis=0)
    jo_rows = iota((8 * chans, 1), 0) // chans
    last_b = cols // 8

    def hidden_step(g):
        f = [feats[r, :, 8 * g : 8 * g + 16, :].reshape(3 * 16, LANES) for r in range(3)]
        u = dot(first_fwd[...], jnp.concatenate(f, axis=0).astype(BF16)) + bias_half
        s = slice(g * 8 * chans, (g + 1) * 8 * chans)
        bh = back_h[s, :]
        if g in (0, last_b):
            fix = fixes[0 if g == 0 else 1]
            bh = jnp.concatenate([bh[0:edge] + fix, bh[edge:]], axis=0)
        a = 1.0 + jnp.tanh(u)
        h = u * a
        b = bh * (a + h * (2.0 - a))
        if g in (0, last_b):
            slot = 8 * g + 1 + jo_rows
            gcol = slot - 2 + col0
            ok = (slot <= cols + 2) & (gcol >= 0) & (gcol < all_cols)
            h = jnp.where(ok, h, 0.0)
            b = jnp.where(ok, b, 0.0)
        h2 = jnp.where(row_ok, h[:, span:], 0.0)
        back_p[s, 0:span] = b[:, 0:span].astype(BF16)
        back_p[s, span:] = jnp.where(row_ok, b[:, span:], 0.0).astype(BF16)
        h = jnp.concatenate([h[:, 0:span], h2], axis=1).astype(BF16)
        hid[0, s, :] = pltpu.roll(h, 1, 1)[:, 0:span]
        hid[1, s, :] = h[:, 0:span]
        hid[2, s, :] = pltpu.roll(h, LANES - 1, 1)[:, 0:span]

    bias_out = jnp.concatenate([bias2[...].T] * GROUP, axis=0)
    groups_c = pl.cdiv(cols, GROUP)

    def back(g, lo):
        q = dot(first_bwd[...], back_p[pl.ds(lo, window), :])
        gm = q[16:32] + pltpu.roll(q[0:16], LANES - 1, 1) + pltpu.roll(q[32:48], 1, 1)
        for ch in range(2):
            grad_maps[ch, GROUP * g : GROUP * (g + 1), :] = gm[8 * ch : 8 * ch + GROUP]

    def taps_of(g):
        lo = g * block
        return jnp.concatenate([hid[r, lo : lo + window, :] for r in range(3)], axis=0)

    def output_step(g):
        both = [k for k in (g, g + 1) if k < groups_c]
        out = dot(fwd[...], jnp.concatenate([taps_of(k) for k in both], axis=1))
        for n_th, k in enumerate(both):
            rows = min(block, (cols - GROUP * k) * chans)
            part = out[0:rows, span * n_th : span * (n_th + 1)] + bias_out[0:rows]
            congestion[k * block : k * block + rows, :] = part.astype(BF16)
            back(k, k * block)

    done = 0
    for g in range(last_b + 1):
        hidden_step(g)
        while done < groups_c and (min(done + 1, groups_c - 1) * GROUP + WINDOW) <= 8 * g:
            output_step(done)
            done += 2
    for g in range(done, groups_c, 2):
        output_step(g)

    kept = grad_maps.shape[1]
    k_rows = iota((kept, 1), 0)
    slot = jnp.where(k_rows < cols, k_rows + 2, 512).astype(F32)
    sources = grad_maps[...].reshape(2 * kept, LANES)[:, 0:NROWS].astype(BF16)
    nets = net_refs[0].shape[2]
    fcol = col0.astype(F32)
    rows = iota((NROWS, nets), 0).astype(F32).astype(BF16)
    one = jnp.ones((), BF16)
    zero = jnp.zeros((), BF16)

    def net_chunk(ref, out, k):
        f, x, y, x0, x1, y1, width, height, cut = relative(ref, k, fcol)
        y0, y1 = y.astype(BF16), y1.astype(BF16)
        in_row = jnp.where((y0 <= rows) & (rows <= y1), one, zero)
        h = dot(sources, in_row)
        in_col = (x0 <= slot) & (slot <= x1)
        s0 = jnp.sum(jnp.where(in_col, h[0:kept], 0.0), axis=0, keepdims=True)
        s1 = jnp.sum(jnp.where(in_col, h[kept:], 0.0), axis=0, keepdims=True)
        out[k, 0:1, :] = s0 / height + s1 / width

    for ref, out in zip(net_refs, grads):
        if ref.shape[0] == 1:
            net_chunk(ref, out, 0)
        else:
            lax.fori_loop(0, ref.shape[0], lambda k, c: (net_chunk(ref, out, k), c)[1], 0)


def shards(
    net_box, net_weight, pin_bin, conv_first, bias_first, conv_second, bias_second, cotangent
):
    cols, chans, span = cotangent.shape
    nets, pins = pin_bin.shape[:2]
    strips = lax.axis_size("strip")
    ncol = lax.axis_size("col")
    cot = cotangent.reshape(cols * chans, span)
    edge = 2 * chans
    one_block = pl.BlockSpec((edge, span), lambda i: (0, 0))
    last_block = pl.BlockSpec((edge, span), lambda i: (cols * chans // edge - 1, 0))

    def full(*shape):
        return pl.BlockSpec(shape, lambda i: (0,) * len(shape))

    to_even, to_odd, plain = pl.pallas_call(
        functools.partial(pack_body, pins),
        grid=(1,),
        in_specs=[full(4, nets), full(1, nets), full(pins, 2, nets), one_block, last_block],
        out_specs=[full(FIELDS + 8, nets), full(FIELDS + 8, nets), full(FIELDS, nets)],
        out_shape=[
            jax.ShapeDtypeStruct((FIELDS + 8, nets), BF16),
            jax.ShapeDtypeStruct((FIELDS + 8, nets), BF16),
            jax.ShapeDtypeStruct((FIELDS, nets), BF16),
        ],
        cost_estimate=cost(10000, 400000),
    )(net_box.T, net_weight.reshape(1, nets), pin_bin.transpose(1, 2, 0), cot, cot)

    def swapped(i, n, phase):
        return (i ^ 1) if phase == 0 else (((i + 1) ^ 1) - 1) % n

    def swap_col(x, phase):
        return lax.ppermute(x, "col", [(i, swapped(i, ncol, phase)) for i in range(ncol)])

    def swap_strip(x, phase):
        pairs = []
        for i in range(strips):
            for c in range(ncol):
                j = swapped(i, strips, phase)
                target = i * ncol + (c ^ 1) if abs(i - j) != 1 else j * ncol + c
                pairs.append((i * ncol + c, target))
        return lax.ppermute(x, ("strip", "col"), pairs)

    few = ncol == 4
    by_even = swap_col(to_even, 0)
    by_odd = swap_col(to_odd, 1)
    opposite = [(i, i ^ 2) for i in range(ncol)]
    if few:
        far = lax.ppermute(plain, "col", opposite)
        groups = [plain[None], by_even[None], by_odd[None], far[None]]
    else:
        groups = [lax.all_gather(plain, "col", axis=0)]
    sides = (by_even[None], by_odd[None])

    cot_to_even, cot_to_odd = call(
        cot_edge_body,
        [
            jax.ShapeDtypeStruct((EDGE, cols * chans), BF16),
            jax.ShapeDtypeStruct((EDGE, cols * chans), BF16),
        ],
        1,
        cost=cost(40000000, 1300000),
    )(lax.optimization_barrier((cot, plain))[0])
    cot_even = swap_strip(cot_to_even, 0)
    cot_odd = swap_strip(cot_to_odd, 1)

    cin = conv_first.shape[3]
    weights = call(
        weight_body,
        [
            jax.ShapeDtypeStruct((GROUP * chans, 3 * WINDOW * chans), BF16),
            jax.ShapeDtypeStruct((3 * GROUP * chans, WINDOW * chans), BF16),
            jax.ShapeDtypeStruct((8 * chans, 9 * 16), BF16),
            jax.ShapeDtypeStruct((48, WINDOW * chans), BF16),
        ],
        2,
        cost=cost(40000000, 1000000),
    )(
        conv_second.reshape(9, chans, chans),
        conv_first.reshape(9, chans, cin).transpose(0, 2, 1),
    )

    hidden_rows = GROUP * pl.cdiv(cols + 2, GROUP) * chans
    own = call(
        functools.partial(back_own_body, chans),
        [jax.ShapeDtypeStruct((hidden_rows, span), F32)] * 2,
        2,
        cost=cost(2000000000, 1000000),
    )(cot, weights[1])
    width = 3 * JCOLS + 2 * edge
    maps, edge_even, edge_odd = call(
        functools.partial(raster_body, pins, cols, span, len(groups)),
        [
            jax.ShapeDtypeStruct((3, JCOLS, LANES), F32),
            jax.ShapeDtypeStruct((EDGE, width), BF16),
            jax.ShapeDtypeStruct((EDGE, width), BF16),
        ],
        len(groups) + 2,
        cost=cost(1500000000, 1500000),
    )(*groups, *sides)

    from_even = swap_strip(edge_even, 0)
    from_odd = swap_strip(edge_odd, 1)

    rows_x = 8 * pl.cdiv(cols + 2, 8) * chans
    back_h = call(
        functools.partial(back_halo_body, chans),
        jax.ShapeDtypeStruct((rows_x, LANES), F32),
        5,
        scratch=[pltpu.VMEM((cols * chans, span), BF16)],
        cost=cost(2000000000, 1000000),
    )(cot_even, cot_odd, weights[1], *own)

    outs = call(
        functools.partial(network_body, pins, len(groups)),
        [jax.ShapeDtypeStruct((cols * chans, span), BF16)]
        + [jax.ShapeDtypeStruct((g.shape[0], 1, nets), F32) for g in groups],
        len(groups) + 12,
        scratch=[
            pltpu.VMEM((3, 3, JCOLS, LANES), F32),
            pltpu.VMEM((3, rows_x, span), BF16),
            pltpu.VMEM((rows_x, LANES), BF16),
            pltpu.VMEM((2, 8 * pl.cdiv(cols + GROUP, 8), LANES), F32),
        ],
        cost=cost(3000000000, 4000000),
    )(
        *groups, maps, from_even, from_odd, back_h, *sides, *weights,
        bias_first.reshape(1, chans), bias_second.reshape(1, chans),
    )
    congestion = outs[0].reshape(cols, chans, span)
    if few:
        own, for_even, for_odd, for_far = outs[1:]
        net_grad = (
            own
            + swap_col(for_even, 0)
            + swap_col(for_odd, 1)
            + lax.ppermute(for_far, "col", opposite)
        )
    else:
        net_grad = lax.psum_scatter(outs[1], "col", scatter_dimension=0, tiled=True)
    return congestion, net_grad.reshape(nets)


def solution(mesh):
    placed = (
        P(("strip", "col"), None),
        P(("strip", "col")),
        P(("strip", "col"), None, None),
        P(),
        P(),
        P(),
        P(),
        P("col", None, "strip"),
    )
    return jax.shard_map(
        shards,
        mesh=mesh,
        in_specs=placed,
        out_specs=(P("col", None, "strip"), P(("strip", "col"))),
        check_vma=False,
    )
```
